32 devices in a mesh: dp: 8 (over z, x), tensor: 4 (over y, core).
Axes of the slice: x: 2, y: 2, z: 4, core: 2. Of those that a mesh axis runs over, the one named last changes fastest.
Arguments:
- inputs: bfloat16 [32, 577, 1024], P('dp', None, 'tensor'), may hold values from -6 to 6
- cotangent: bfloat16 [32, 577, 1024], P('dp', None, 'tensor'), may hold values from -6 to 6
- slot_mask: int32 [32], P('dp'), may hold values from 0 to 1, as said below
- w_qkv: bfloat16 [3, 1024, 1024], P(None, None, 'tensor'), may hold values from -0.1875 to 0.1875
- bias_qv: bfloat16 [2, 1024], P(None, 'tensor'), may hold values from -3 to 3
- w_out: bfloat16 [1024, 1024], P('tensor'), may hold values from -2 to 2
- bias_out: bfloat16 [1024], replicated, may hold values from -3 to 3
- ln1_gain: bfloat16 [1024], replicated, may hold values from 0.25 to 1.75
- ln1_bias: bfloat16 [1024], replicated, may hold values from -2 to 2
- ln2_gain: bfloat16 [1024], replicated, may hold values from 0.25 to 1.75
- ln2_bias: bfloat16 [1024], replicated, may hold values from -2 to 2
- w_up: bfloat16 [1024, 4096], P(None, 'tensor'), may hold values from -0.1875 to 0.1875
- bias_up: bfloat16 [4096], P('tensor'), may hold values from -3 to 3
- w_down: bfloat16 [4096, 1024], P('tensor'), may hold values from -0.09375 to 0.09375
- bias_down: bfloat16 [1024], replicated, may hold values from -3 to 3
Outputs:
- layer_out: bfloat16 [32, 577, 1024], P('dp', None, 'tensor')
- input_grad: bfloat16 [32, 577, 1024], P('dp', None, 'tensor')
- grad_qkv: float32 [3, 1024, 1024], P(None, None, 'tensor')
- grad_bias_qv: float32 [2, 1024], P(None, 'tensor')
- grad_out: float32 [1024, 1024], P('tensor')
- grad_bias_out: float32 [1024], replicated
- grad_ln1_gain: float32 [1024], replicated
- grad_ln1_bias: float32 [1024], replicated
- grad_ln2_gain: float32 [1024], replicated
- grad_ln2_bias: float32 [1024], replicated
- grad_up: float32 [1024, 4096], P(None, 'tensor')
- grad_bias_up: float32 [4096], P('tensor')
- grad_down: float32 [4096, 1024], P('tensor')
- grad_bias_down: float32 [1024], replicated
The draws below stay inside these ranges and needn't reach their ends.
Inputs may be any that keep to these rules, and one draw needn't show every extreme that they name: `slot_mask`: exactly 28 of the 32 entries are 1.
All inputs are finite; a program needn't handle non-finite values.
Results may differ from the reference program's by a relative error of at most 0.012.
The reference program's roundings to bfloat16 on the way count: a program that leaves them out, or rounds other values in their place, can miss the bound.
Values may be sent and summed in bfloat16 or wider, within the bound.
No kernel may reach another device: no remote copies, remote signals or barrier semaphores. Data moves between devices by JAX's collectives and lax.ppermute only.
A program may use at most 256 MiB of HBM per device.

```python
import jax
import jax.numpy as jnp
from jax import lax

D = 1024
HEADS = 16
HEAD = 64
FF = 4096
SEQ = 577
SLOTS = 32
IMAGES = 28


def draw_slot_mask(key, part):
    order = jax.random.permutation(key, SLOTS)
    return (order < IMAGES).astype(jnp.int32)


def block_scale(stream_key, extent, cuts, smallest, high):
    factor_of, own = 1.0, jax.random.fold_in(stream_key, 6)
    for position, shards_of in cuts:
        steps = jnp.exp(jax.random.uniform(jax.random.fold_in(own, position), (shards_of,), jnp.float32, smallest / len(cuts), high / len(cuts)))
        factor_of = factor_of * jnp.repeat(steps, extent[position] // shards_of).reshape([-1 if axis == position else 1 for axis in range(len(extent))])
    return factor_of


def gaussian(stream_key, dims, scale, limit, cuts=(), kind=jnp.bfloat16):
    array = scale * jax.random.normal(stream_key, dims, jnp.float32)
    if cuts:
        array = array * block_scale(stream_key, dims, cuts, -0.22, 0.18)
    return jnp.clip(array, -limit, limit).astype(kind)


def setup_inputs(seed: int = 0) -> dict:
    streams_of = jax.random.split(jax.random.key(seed), 16)
    return {
        "inputs": gaussian(streams_of[0], (SLOTS, SEQ, D), 1.0, 6.0, ((0, 8), (2, 4))),
        "cotangent": gaussian(streams_of[1], (SLOTS, SEQ, D), 1.0, 6.0, ((0, 8), (2, 4))),
        "slot_mask": draw_slot_mask(jax.random.fold_in(streams_of[15], 71), 0),
        "w_qkv": gaussian(streams_of[3], (3, D, D), D ** -0.5, 0.1875, ((2, 4),)),
        "bias_qv": gaussian(streams_of[4], (2, D), 0.5, 3.0, ((1, 4),)),
        "w_out": gaussian(streams_of[5], (D, D), 8 ** -0.5, 2.0, ((0, 4),)),
        "bias_out": gaussian(streams_of[6], (D,), 0.5, 3.0),
        "ln1_gain": jnp.clip(1.0 + 0.15 * jax.random.normal(streams_of[7], (D,), jnp.float32), 0.25, 1.75).astype(jnp.bfloat16),
        "ln1_bias": gaussian(streams_of[8], (D,), 0.3, 2.0),
        "ln2_gain": jnp.clip(1.0 + 0.15 * jax.random.normal(streams_of[9], (D,), jnp.float32), 0.25, 1.75).astype(jnp.bfloat16),
        "ln2_bias": gaussian(streams_of[10], (D,), 0.3, 2.0),
        "w_up": gaussian(streams_of[11], (D, FF), D ** -0.5, 0.1875, ((1, 4),)),
        "bias_up": gaussian(streams_of[12], (FF,), 0.5, 3.0, ((0, 4),)),
        "w_down": gaussian(streams_of[13], (FF, D), FF ** -0.5, 0.09375, ((0, 4),)),
        "bias_down": gaussian(streams_of[14], (D,), 0.5, 3.0),
    }


@jax.custom_vjp
def low(v):
    return lax.optimization_barrier(v.astype(jnp.bfloat16)).astype(jnp.float32)

@jax.custom_vjp
def low_back(v):
    return v

def low_keep(v):
    return (low(v), None)

def low_pass(kept, grad):
    return (grad,)

def back_keep(v):
    return (v, None)

def back_low(kept, grad):
    return (low(grad),)
low.defvjp(low_keep, low_pass)
low_back.defvjp(back_keep, back_low)
EPS = 1e-05
GELU_K = 1.702
HIGH = lax.Precision.HIGHEST

def layer_norm(rows, gain, shift):
    center = rows - lax.optimization_barrier(jnp.mean(rows, axis=-1, keepdims=True))
    spread = lax.optimization_barrier(jnp.mean(center * center, axis=-1, keepdims=True))
    return center * lax.rsqrt(spread + EPS) * gain + shift

def forward(rows, params):
    w_qkv, bias_qv, w_out, bias_out, gain_one, shift_one, gain_two, shift_two, w_up, bias_up, w_down, bias_down = params
    normed = low(layer_norm(rows, gain_one, shift_one))
    query = low(low_back((jnp.dot(normed, w_qkv[0], precision=HIGH) + bias_qv[0]) * 0.125))
    keys = low(low_back(jnp.dot(normed, w_qkv[1], precision=HIGH)))
    values = low(low_back(jnp.dot(normed, w_qkv[2], precision=HIGH) + bias_qv[1]))
    split = (SEQ, HEADS, HEAD)
    scores = low_back(jnp.einsum('qhe,khe->hqk', query.reshape(split), keys.reshape(split), precision=HIGH))
    expo = jnp.exp(scores - lax.optimization_barrier(jnp.max(scores, axis=-1, keepdims=True)))
    probs = low(expo / lax.optimization_barrier(jnp.sum(expo, axis=-1, keepdims=True)))
    attended = jnp.einsum('hqk,khe->qhe', probs, values.reshape(split), precision=HIGH).reshape(SEQ, D)
    attended = low(low_back(attended))
    resid = rows + low_back(jnp.dot(attended, w_out, precision=HIGH) + bias_out)
    normed_two = low(layer_norm(resid, gain_two, shift_two))
    hidden = low_back(jnp.dot(normed_two, w_up, precision=HIGH) + bias_up)
    active = low(hidden * jax.nn.sigmoid(GELU_K * hidden))
    return resid + low_back(jnp.dot(active, w_down, precision=HIGH) + bias_down)

def reference(inputs, cotangent, slot_mask, w_qkv, bias_qv, w_out, bias_out, ln1_gain, ln1_bias, ln2_gain, ln2_bias, w_up, bias_up, w_down, bias_down):
    params = tuple((item.astype(jnp.float32) for item in (w_qkv, bias_qv, w_out, bias_out, ln1_gain, ln1_bias, ln2_gain, ln2_bias, w_up, bias_up, w_down, bias_down)))

    def one_image(totals, item):
        rows, grad_rows, live = item
        out_rows, pull = jax.vjp(forward, rows.astype(jnp.float32), params)
        grad_in, grad_params = pull(grad_rows.astype(jnp.float32) * live.astype(jnp.float32))
        totals = jax.tree.map(lambda left, right: left + right, totals, grad_params)
        return (totals, (out_rows.astype(jnp.bfloat16), grad_in.astype(jnp.bfloat16)))
    zeros = jax.tree.map(jnp.zeros_like, params)
    totals, outputs = lax.scan(one_image, zeros, (inputs, cotangent, slot_mask))
    layer_out, input_grad = outputs
    grad_qkv, grad_bias_qv, grad_out, grad_bias_out, grad_ln1_gain, grad_ln1_bias, grad_ln2_gain, grad_ln2_bias, grad_up, grad_bias_up, grad_down, grad_bias_down = totals
    return (layer_out, input_grad, grad_qkv, grad_bias_qv, grad_out, grad_bias_out, grad_ln1_gain, grad_ln1_bias, grad_ln2_gain, grad_ln2_bias, grad_up, grad_bias_up, grad_down, grad_bias_down)
```

```python
import functools

import jax
import jax.numpy as jnp
from jax import lax
from jax.experimental import pallas as pl
from jax.experimental.pallas import tpu as pltpu
from jax.sharding import PartitionSpec as P

HEAD = 64
LANES = 128
ROW_TILE = 16
EPS = 1e-05
GELU_K = 1.702
FAR = -1e30

F32 = jnp.float32
BF16 = jnp.bfloat16

NT = (((1,), (1,)), ((), ()))
NN = (((1,), (0,)), ((), ()))
TN = (((0,), (0,)), ((), ()))


def mm(left, right, dims):
    return lax.dot_general(left, right, dims, preferred_element_type=F32)


def head_views(half, seq, q, k):
    lane = lax.broadcasted_iota(jnp.int32, q.shape, 1)
    row = lax.broadcasted_iota(jnp.int32, q.shape, 0)
    mine = (lane >= HEAD) if half else (lane < HEAD)
    spare = lane == (0 if half else HEAD)
    zero = jnp.zeros_like(q)
    q_only = jnp.where(mine, q, zero)
    k_only = jnp.where(mine, k, zero)
    q_mask = jnp.where(spare, jnp.ones_like(q), q_only)
    far = jnp.full_like(k, FAR)
    k_mask = jnp.where(spare & (row >= seq), far, k_only)
    return mine, q_only, k_only, q_mask, k_mask


def attn_fwd_kernel(seq, q_ref, k_ref, v_ref, o_ref, lse_ref):
    q, k, v = q_ref[...], k_ref[...], v_ref[...]
    v_t = v.T
    pieces = []
    for half in range(2):
        _, _, _, q_mask, k_mask = head_views(half, seq, q, k)
        s_t = mm(k_mask, q_mask, NT)
        peak = jnp.max(s_t, axis=0, keepdims=True)
        expo = jnp.exp(s_t - peak)
        total = jnp.sum(expo, axis=0, keepdims=True)
        p_t = (expo * (1.0 / total)).astype(BF16)
        pieces.append(mm(v_t[half * HEAD : (half + 1) * HEAD], p_t, NN))
        lse_ref[0, 0, half : half + 1, :] = peak + jnp.log(total)
    o_ref[...] = jnp.concatenate(pieces, axis=0).T.astype(BF16)


def attn_bwd_kernel(seq, q_ref, k_ref, v_ref, do_ref, lse_ref, dq_ref, dk_ref, dv_ref):
    q, k, v, do = q_ref[...], k_ref[...], v_ref[...], do_ref[...]
    k_t = k.T
    dq_t, dk, dv = [], None, None
    for half in range(2):
        mine, q_only, _, q_mask, k_mask = head_views(half, seq, q, k)
        do_only = jnp.where(mine, do, jnp.zeros_like(do))
        s_t = mm(k_mask, q_mask, NT)
        p_t = jnp.exp(s_t - lse_ref[0, 0, half : half + 1, :])
        dp_t = mm(v, do_only, NT)
        inner = jnp.sum(p_t * dp_t, axis=0, keepdims=True)
        ds_t = (p_t * (dp_t - inner)).astype(BF16)
        dv_half = mm(p_t.astype(BF16), do_only, NN)
        dk_half = mm(ds_t, q_only, NN)
        dq_t.append(mm(k_t[half * HEAD : (half + 1) * HEAD], ds_t, NN))
        dv = dv_half if dv is None else dv + dv_half
        dk = dk_half if dk is None else dk + dk_half
    dq_ref[...] = jnp.concatenate(dq_t, axis=0).T.astype(BF16) * 0.125
    dk_ref[...] = dk.astype(BF16)
    dv_ref[...] = dv.astype(BF16)


def attention_forward(q, k, v, images, seq):
    rows, width = q.shape
    s = rows // images
    pairs = width // LANES
    block = pl.BlockSpec((s, LANES), lambda i, j: (i, j))
    lse_block = pl.BlockSpec((1, 1, 2, s), lambda i, j: (i, j, 0, 0))
    n = images * pairs * 2
    return pl.pallas_call(
        functools.partial(attn_fwd_kernel, seq),
        grid=(images, pairs),
        in_specs=[block] * 3,
        out_specs=[block, lse_block],
        out_shape=[
            jax.ShapeDtypeStruct((rows, width), BF16),
            jax.ShapeDtypeStruct((images, pairs, 2, s), F32),
        ],
        cost_estimate=pl.CostEstimate(
            flops=n * 4 * s * s * 256, bytes_accessed=rows * width * 8, transcendentals=n * s * s
        ),
        name="attn_fwd",
    )(q, k, v)


def attention_backward(q, k, v, do, lse, images, seq):
    rows, width = q.shape
    s = rows // images
    pairs = width // LANES
    block = pl.BlockSpec((s, LANES), lambda i, j: (i, j))
    lse_block = pl.BlockSpec((1, 1, 2, s), lambda i, j: (i, j, 0, 0))
    n = images * pairs * 2
    return pl.pallas_call(
        functools.partial(attn_bwd_kernel, seq),
        grid=(images, pairs),
        in_specs=[block] * 4 + [lse_block],
        out_specs=[block] * 3,
        out_shape=[jax.ShapeDtypeStruct((rows, width), BF16)] * 3,
        cost_estimate=pl.CostEstimate(
            flops=n * 10 * s * s * 256, bytes_accessed=rows * width * 14, transcendentals=n * s * s
        ),
        name="attn_bwd",
    )(q, k, v, do, lse)


def norm_stats(rows):
    mean = jnp.mean(rows, axis=-1, keepdims=True)
    center = rows - mean
    inv = lax.rsqrt(jnp.mean(center * center, axis=-1, keepdims=True) + EPS)
    return mean, inv


def norm_back(grad, unit, inv, gain):
    scaled = grad * gain
    first = jnp.mean(scaled, axis=-1, keepdims=True)
    second = jnp.mean(scaled * unit, axis=-1, keepdims=True)
    return (
        inv * (scaled - first - unit * second),
        jnp.sum(grad * unit, axis=0),
        jnp.sum(grad, axis=0),
    )


def pick(pieces, index):
    out = pieces[0]
    for n in range(1, len(pieces)):
        out = jnp.where(index == n, pieces[n], out)
    return out


def per_device(
    inputs,
    cotangent,
    slot_mask,
    w_qkv,
    bias_qv,
    w_out,
    bias_out,
    ln1_gain,
    ln1_bias,
    ln2_gain,
    ln2_bias,
    w_up,
    bias_up,
    w_down,
    bias_down,
):
    n_img, seq, width = inputs.shape
    n_tensor = lax.axis_size("tensor")
    n_dp = lax.axis_size("dp")
    chips = n_tensor // 2
    images = n_img // chips
    full = width * n_tensor
    padded = -(-seq // ROW_TILE) * ROW_TILE
    rows = images * padded
    t_idx = lax.axis_index("tensor")
    d_idx = lax.axis_index("dp")
    chip, core = t_idx // 2, t_idx % 2
    bits = n_dp.bit_length() - 1

    def chip_shift(value, step):
        perm = [
            (2 * a + b, 2 * ((a + step) % chips) + b) for a in range(chips) for b in range(2)
        ]
        return lax.ppermute(value, "tensor", perm)

    def core_swap(value):
        return lax.ppermute(value, "tensor", [(a, a ^ 1) for a in range(n_tensor)])

    def dp_swap(value, bit):
        return lax.ppermute(value, "dp", [(a, a ^ (1 << bit)) for a in range(n_dp)])

    def my_images(value, step):
        return lax.dynamic_slice_in_dim(value, ((chip + step) % chips) * images, images, 0)

    def gather_rows(value):
        mine = [my_images(value, 0)] + [
            chip_shift(my_images(value, step), step) for step in range(1, chips)
        ]
        theirs = [core_swap(piece) for piece in mine]
        parts = []
        for a in range(chips):
            which = (chip - a) % chips
            own, other = pick(mine, which), pick(theirs, which)
            parts += [jnp.where(core == 0, own, other), jnp.where(core == 0, other, own)]
        out = jnp.concatenate(parts, axis=2)
        out = jnp.pad(out, ((0, 0), (0, padded - seq), (0, 0)))
        return out.reshape(rows, full)

    def scatter_rows(value):
        value = value.reshape(images, padded, full)[:, :seq]
        pieces = []
        for step in range(chips):
            block = 2 * ((chip + step) % chips) + core
            piece = pick(
                [value[:, :, n * width : (n + 1) * width] for n in range(n_tensor)], block
            )
            pieces.append(piece if step == 0 else chip_shift(piece, step))
        return jnp.concatenate([pick(pieces, (chip - a) % chips) for a in range(chips)], axis=0)

    side = d_idx & 1

    def gather_weight(weight, axis):
        half = weight.shape[axis] // 2
        blocks = [weight]
        send = lax.dynamic_slice_in_dim(weight, side * half, half, axis)
        for step in range(1, chips):
            got = chip_shift(send, step)
            other = dp_swap(got, 0)
            blocks.append(
                jnp.where(
                    side == 0,
                    jnp.concatenate([got, other], axis),
                    jnp.concatenate([other, got], axis),
                )
            )
        return blocks

    def reduce_blocks(blocks):
        total = blocks[0].astype(F32)
        for step in range(1, chips):
            total = total + chip_shift(blocks[step].astype(BF16), chips - step).astype(F32)
        total = total.astype(BF16)
        for bit in range(bits):
            half = total.shape[0] // 2
            at = (d_idx >> bit) & 1
            keep = lax.dynamic_slice_in_dim(total, at * half, half, 0)
            send = lax.dynamic_slice_in_dim(total, (1 - at) * half, half, 0)
            total = (keep.astype(F32) + dp_swap(send, bit).astype(F32)).astype(BF16)
        for bit in reversed(range(bits)):
            at = (d_idx >> bit) & 1
            other = dp_swap(total, bit)
            total = jnp.where(
                at == 0,
                jnp.concatenate([total, other], 0),
                jnp.concatenate([other, total], 0),
            )
        return total.astype(F32)

    def exchange(part):
        part = part.astype(BF16)
        return part.astype(F32) + core_swap(part).astype(F32)

    gain_one, shift_one = ln1_gain.astype(F32), ln1_bias.astype(F32)
    gain_two, shift_two = ln2_gain.astype(F32), ln2_bias.astype(F32)

    x = gather_rows(inputs)
    wq = gather_weight(w_qkv, 1)
    small = jnp.concatenate([bias_up, bias_qv.reshape(-1)])
    smalls = [small] + [chip_shift(small, step) for step in range(1, chips)]
    n_up = bias_up.shape[0]
    up_bias = [v[:n_up].astype(F32) for v in smalls]
    qv_bias = [v[n_up:].reshape(2, width).astype(F32) for v in smalls]
    wo = gather_weight(w_out, 0)
    wu = gather_weight(w_up, 0)
    live = my_images(slot_mask, 0).astype(BF16)[:, None, None]
    dy = gather_rows(cotangent)
    dy = (dy.reshape(images, padded, full) * live).reshape(rows, full)
    wd = gather_weight(w_down, 0)

    x32 = x.astype(F32)
    mean_one, inv_one = norm_stats(x32)
    unit_one = (x32 - mean_one) * inv_one
    normed_one = (unit_one * gain_one + shift_one).astype(BF16)
    saved = []
    attn_part = None
    for r in range(chips):
        q = ((mm(normed_one, wq[r][0], NN) + qv_bias[r][0]) * 0.125).astype(BF16)
        k = mm(normed_one, wq[r][1], NN).astype(BF16)
        v = (mm(normed_one, wq[r][2], NN) + qv_bias[r][1]).astype(BF16)
        o, lse = attention_forward(q, k, v, images, seq)
        saved.append((q, k, v, o, lse))
        part = mm(o, wo[r], NN)
        attn_part = part if attn_part is None else attn_part + part
    resid = x32 + (exchange(attn_part) + bias_out.astype(F32))
    mean_two, inv_two = norm_stats(resid)
    unit_two = (resid - mean_two) * inv_two
    normed_two = (unit_two * gain_two + shift_two).astype(BF16)
    mlp_part = None
    acts, slopes = [], []
    for r in range(chips):
        hidden = mm(normed_two, wu[r], NN) + up_bias[r]
        sigma = jax.nn.sigmoid(GELU_K * hidden)
        acts.append((hidden * sigma).astype(BF16))
        slopes.append(sigma + GELU_K * hidden * sigma * (1.0 - sigma))
        part = mm(acts[r], wd[r], NN)
        mlp_part = part if mlp_part is None else mlp_part + part
    out = (resid + (exchange(mlp_part) + bias_down.astype(F32))).astype(BF16)
    layer_out = scatter_rows(out)

    grad_down = reduce_blocks([mm(acts[r], dy, TN) for r in range(chips)])
    d_hidden = []
    part_two = None
    for r in range(chips):
        d_hidden.append((mm(dy, wd[r], NT) * slopes[r]).astype(BF16))
        part = mm(d_hidden[r], wu[r], NT)
        part_two = part if part_two is None else part_two + part
    grad_up = reduce_blocks([mm(normed_two, d_hidden[r], TN) for r in range(chips)])
    back_two, g_gain_two, g_shift_two = norm_back(exchange(part_two), unit_two, inv_two, gain_two)
    d_resid = dy.astype(F32) + back_two
    d_attn = d_resid.astype(BF16)
    part_one = None
    attn_blocks = []
    bqv_blocks = []
    for r in range(chips):
        q, k, v, o, lse = saved[r]
        do = mm(d_attn, wo[r], NT).astype(BF16)
        grads = attention_backward(q, k, v, do, lse, images, seq)
        for n in range(3):
            part = mm(grads[n], wq[r][n], NT)
            part_one = part if part_one is None else part_one + part
        attn_blocks.append(
            jnp.concatenate(
                [mm(normed_one, g, TN) for g in grads] + [mm(d_attn, o, TN)], axis=0
            )
        )
        bqv_blocks.append(
            jnp.concatenate([jnp.sum(grads[n], axis=0, dtype=F32) for n in (0, 2)])
        )
    grad_attn = reduce_blocks(attn_blocks)
    back_one, g_gain_one, g_shift_one = norm_back(exchange(part_one), unit_one, inv_one, gain_one)
    input_grad = scatter_rows((d_resid + back_one).astype(BF16))
    grad_qkv = grad_attn[: 3 * full].reshape(3, full, width)
    grad_out = grad_attn[3 * full :].T

    shared = jnp.concatenate(
        [
            jnp.sum(d_attn, axis=0, dtype=F32),
            g_gain_one,
            g_shift_one,
            g_gain_two,
            g_shift_two,
            jnp.sum(dy, axis=0, dtype=F32),
        ]
    )
    shared = jnp.where(core == 0, shared, 0.0)
    own = [
        jnp.concatenate([jnp.sum(d_hidden[r], axis=0, dtype=F32), bqv_blocks[r]])
        for r in range(chips)
    ]
    placed = []
    for n in range(n_tensor):
        here = pick(own, (chip - n // 2) % chips)
        placed.append(jnp.where(core == n % 2, here, 0.0))
    vector = lax.psum(jnp.concatenate([shared] + placed), ("dp", "tensor"))
    vecs = [vector[n * full : (n + 1) * full] for n in range(6)]
    size = n_up + 2 * width
    mine = pick(
        [vector[6 * full + n * size : 6 * full + (n + 1) * size] for n in range(n_tensor)], t_idx
    )
    return (
        layer_out,
        input_grad,
        grad_qkv,
        mine[n_up:].reshape(2, width),
        grad_out,
        vecs[0],
        vecs[1],
        vecs[2],
        vecs[3],
        vecs[4],
        grad_up,
        mine[:n_up],
        grad_down,
        vecs[5],
    )


def solution(mesh):
    return jax.shard_map(
        per_device,
        mesh=mesh,
        in_specs=(
            P("dp", None, "tensor"),
            P("dp", None, "tensor"),
            P("dp"),
            P(None, None, "tensor"),
            P(None, "tensor"),
            P("tensor", None),
            P(),
            P(),
            P(),
            P(),
            P(),
            P(None, "tensor"),
            P("tensor"),
            P("tensor", None),
            P(),
        ),
        out_specs=(
            P("dp", None, "tensor"),
            P("dp", None, "tensor"),
            P(None, None, "tensor"),
            P(None, "tensor"),
            P("tensor", None),
            P(),
            P(),
            P(),
            P(),
            P(),
            P(None, "tensor"),
            P("tensor"),
            P("tensor", None),
            P(),
        ),
        check_vma=False,
    )
```

```python
import functools

import jax
import jax.numpy as jnp
from jax import lax
from jax.experimental import pallas as pl
from jax.experimental.pallas import tpu as pltpu
from jax.sharding import PartitionSpec as P

HEAD = 64
LANES = 128
ROW_TILE = 16
EPS = 1e-05
GELU_K = 1.702
FAR = -1e30

F32 = jnp.float32
BF16 = jnp.bfloat16

NT = (((1,), (1,)), ((), ()))
NN = (((1,), (0,)), ((), ()))
TN = (((0,), (0,)), ((), ()))


def mm(left, right, dims):
    return lax.dot_general(left, right, dims, preferred_element_type=F32)


def head_views(half, seq, q, k):
    lane = lax.broadcasted_iota(jnp.int32, q.shape, 1)
    row = lax.broadcasted_iota(jnp.int32, q.shape, 0)
    mine = (lane >= HEAD) if half else (lane < HEAD)
    spare = lane == (0 if half else HEAD)
    zero = jnp.zeros_like(q)
    q_only = jnp.where(mine, q, zero)
    k_only = jnp.where(mine, k, zero)
    q_mask = jnp.where(spare, jnp.ones_like(q), q_only)
    far = jnp.full_like(k, FAR)
    k_mask = jnp.where(spare & (row >= seq), far, k_only)
    return mine, q_only, k_only, q_mask, k_mask


def attn_fwd_kernel(seq, q_ref, k_ref, v_ref, o_ref, lse_ref):
    q, k, v = q_ref[...], k_ref[...], v_ref[...]
    v_t = v.T
    pieces = []
    for half in range(2):
        _, _, _, q_mask, k_mask = head_views(half, seq, q, k)
        s_t = mm(k_mask, q_mask, NT)
        peak = jnp.max(s_t, axis=0, keepdims=True)
        expo = jnp.exp(s_t - peak)
        total = jnp.sum(expo, axis=0, keepdims=True)
        p_t = (expo * (1.0 / total)).astype(BF16)
        pieces.append(mm(v_t[half * HEAD : (half + 1) * HEAD], p_t, NN))
        lse_ref[0, 0, half : half + 1, :] = peak + jnp.log(total)
    o_ref[...] = jnp.concatenate(pieces, axis=0).T.astype(BF16)


def attn_bwd_kernel(seq, width, q_ref, k_ref, v_ref, do_ref, lse_ref, grads_ref):
    q, k, v, do = q_ref[...], k_ref[...], v_ref[...], do_ref[...]
    k_t = k.T
    dq_t, dk, dv = [], None, None
    for half in range(2):
        mine, q_only, _, q_mask, k_mask = head_views(half, seq, q, k)
        do_only = jnp.where(mine, do, jnp.zeros_like(do))
        s_t = mm(k_mask, q_mask, NT)
        p_t = jnp.exp(s_t - lse_ref[0, 0, half : half + 1, :])
        dp_t = mm(v, do_only, NT)
        inner = jnp.sum(p_t * dp_t, axis=0, keepdims=True)
        ds_t = (p_t * (dp_t - inner)).astype(BF16)
        dv_half = mm(p_t.astype(BF16), do_only, NN)
        dk_half = mm(ds_t, q_only, NN)
        dq_t.append(mm(k_t[half * HEAD : (half + 1) * HEAD], ds_t, NN))
        dv = dv_half if dv is None else dv + dv_half
        dk = dk_half if dk is None else dk + dk_half
    dq = jnp.concatenate(dq_t, axis=0).T.astype(BF16) * 0.125
    for n, grad in enumerate((dq, dk.astype(BF16), dv.astype(BF16))):
        at = pl.multiple_of(n * width + pl.program_id(1) * LANES, LANES)
        grads_ref[:, pl.ds(at, LANES)] = grad


def column_blocks(s, pairs, parts):
    def at(part):
        return pl.BlockSpec((s, LANES), lambda i, j: (i, part * pairs + j))

    return [at(part) for part in range(parts)]


def attention_forward(qkv, images, seq):
    rows, width = qkv.shape[0], qkv.shape[1] // 3
    s = rows // images
    pairs = width // LANES
    block = pl.BlockSpec((s, LANES), lambda i, j: (i, j))
    lse_block = pl.BlockSpec((1, 1, 2, s), lambda i, j: (i, j, 0, 0))
    n = images * pairs * 2
    return pl.pallas_call(
        functools.partial(attn_fwd_kernel, seq),
        grid=(images, pairs),
        in_specs=column_blocks(s, pairs, 3),
        out_specs=[block, lse_block],
        out_shape=[
            jax.ShapeDtypeStruct((rows, width), BF16),
            jax.ShapeDtypeStruct((images, pairs, 2, s), F32),
        ],
        cost_estimate=pl.CostEstimate(
            flops=n * 4 * s * s * 256, bytes_accessed=rows * width * 8, transcendentals=n * s * s
        ),
        name="attn_fwd",
    )(qkv, qkv, qkv)


def attention_backward(qkv, do, lse, images, seq):
    rows, width = do.shape
    s = rows // images
    pairs = width // LANES
    block = pl.BlockSpec((s, LANES), lambda i, j: (i, j))
    lse_block = pl.BlockSpec((1, 1, 2, s), lambda i, j: (i, j, 0, 0))
    n = images * pairs * 2
    return pl.pallas_call(
        functools.partial(attn_bwd_kernel, seq, width),
        grid=(images, pairs),
        in_specs=column_blocks(s, pairs, 3) + [block, lse_block],
        out_specs=pl.BlockSpec((s, 3 * width), lambda i, j: (i, 0)),
        out_shape=jax.ShapeDtypeStruct((rows, 3 * width), BF16),
        cost_estimate=pl.CostEstimate(
            flops=n * 10 * s * s * 256, bytes_accessed=rows * width * 14, transcendentals=n * s * s
        ),
        name="attn_bwd",
    )(qkv, qkv, qkv, do, lse)


def norm_stats(rows):
    mean = jnp.mean(rows, axis=-1, keepdims=True)
    center = rows - mean
    inv = lax.rsqrt(jnp.mean(center * center, axis=-1, keepdims=True) + EPS)
    return mean, inv


def norm_back(grad, unit, inv, gain):
    scaled = grad * gain
    first = jnp.mean(scaled, axis=-1, keepdims=True)
    second = jnp.mean(scaled * unit, axis=-1, keepdims=True)
    return (
        inv * (scaled - first - unit * second),
        jnp.sum(grad * unit, axis=0),
        jnp.sum(grad, axis=0),
    )


def pick(pieces, index):
    out = pieces[0]
    for n in range(1, len(pieces)):
        out = jnp.where(index == n, pieces[n], out)
    return out


def per_device(
    inputs,
    cotangent,
    slot_mask,
    w_qkv,
    bias_qv,
    w_out,
    bias_out,
    ln1_gain,
    ln1_bias,
    ln2_gain,
    ln2_bias,
    w_up,
    bias_up,
    w_down,
    bias_down,
):
    n_img, seq, width = inputs.shape
    n_tensor = lax.axis_size("tensor")
    n_dp = lax.axis_size("dp")
    chips = n_tensor // 2
    images = n_img // chips
    full = width * n_tensor
    padded = -(-seq // ROW_TILE) * ROW_TILE
    split = images % 2 == 0
    near = images // 2 if split else images
    local = near * padded
    t_idx = lax.axis_index("tensor")
    d_idx = lax.axis_index("dp")
    chip, core = t_idx // 2, t_idx % 2
    bits = n_dp.bit_length() - 1
    side = d_idx & 1
    steps = range(1, chips)

    def chip_shift(value, step):
        perm = [
            (2 * a + b, 2 * ((a + step) % chips) + b) for a in range(chips) for b in range(2)
        ]
        return lax.ppermute(value, "tensor", perm)

    def core_swap(value):
        return lax.ppermute(value, "tensor", [(a, a ^ 1) for a in range(n_tensor)])

    def dp_swap(value, bit):
        return lax.ppermute(value, "dp", [(a, a ^ (1 << bit)) for a in range(n_dp)])

    def my_images(value, step):
        return lax.dynamic_slice_in_dim(value, ((chip + step) % chips) * images, images, 0)

    def by_core(first, second):
        return jnp.where(core == 0, first, second)

    def fetch_rows(value):
        return [chip_shift(my_images(value, step), step) for step in steps]

    def core_rows(value, arrived):
        mine = [my_images(value, 0)] + arrived
        theirs = []
        for n, piece in enumerate(mine):
            if split:
                theirs.append(core_swap(by_core(piece[near:], piece[:near])))
                mine[n] = by_core(piece[:near], piece[near:])
            else:
                theirs.append(core_swap(piece))
        parts = []
        for a in range(chips):
            which = (chip - a) % chips
            own, other = pick(mine, which), pick(theirs, which)
            parts += [by_core(own, other), by_core(other, own)]
        out = jnp.concatenate(parts, axis=2)
        out = jnp.pad(out, ((0, 0), (0, padded - seq), (0, 0)))
        return out.reshape(local, full)

    def complete(rows):
        return jnp.concatenate([rows, core_swap(rows)], axis=0) if split else rows

    def exchange(part):
        part = part.astype(BF16)
        return part[:local].astype(F32) + core_swap(part[-local:]).astype(F32)

    def scatter_rows(value):
        value = value.reshape(near, padded, full)[:, :seq]
        cols = [value[:, :, n * width : (n + 1) * width] for n in range(n_tensor)]
        keep = [by_core(cols[2 * a], cols[2 * a + 1]) for a in range(chips)]
        if split:
            give = [by_core(cols[2 * a + 1], cols[2 * a]) for a in range(chips)]
            got = core_swap(jnp.concatenate(give, axis=2))
            got = [got[:, :, a * width : (a + 1) * width] for a in range(chips)]
            keep = [
                jnp.concatenate([by_core(m, g), by_core(g, m)], axis=0)
                for m, g in zip(keep, got)
            ]
        pieces = [pick(keep, chip)]
        for step in steps:
            pieces.append(chip_shift(pick(keep, (chip + step) % chips), step))
        return jnp.concatenate([pick(pieces, (chip - a) % chips) for a in range(chips)], axis=0)

    def fetch_weight(weight):
        half = weight.shape[0] // 2
        send = lax.dynamic_slice_in_dim(weight, side * half, half, 0)
        return [chip_shift(send, step) for step in steps]

    def whole_weight(weight, arrived):
        blocks = [weight]
        for got in arrived:
            other = dp_swap(got, 0)
            blocks.append(
                jnp.where(
                    side == 0,
                    jnp.concatenate([got, other], 0),
                    jnp.concatenate([other, got], 0),
                )
            )
        return blocks

    def halves(value, bit):
        half = value.shape[0] // 2
        at = (d_idx >> bit) & 1
        keep = lax.dynamic_slice_in_dim(value, at * half, half, 0)
        send = lax.dynamic_slice_in_dim(value, (1 - at) * half, half, 0)
        return keep, send

    def reduce_blocks(blocks, dp_first):
        first = 0
        if dp_first:
            cut = [halves(block, 0) for block in blocks]
            got = yield [dp_swap(jnp.concatenate([c[1] for c in cut], 0), 0)]
            size = cut[0][0].shape[0]
            blocks = [
                (c[0].astype(F32) + got[0][n * size : (n + 1) * size].astype(F32)).astype(BF16)
                for n, c in enumerate(cut)
            ]
            first = 1
        got = yield [chip_shift(blocks[step], chips - step) for step in steps]
        total = blocks[0].astype(F32)
        for piece in got:
            total = total + piece.astype(F32)
        total = total.astype(BF16)
        for bit in range(first, bits):
            keep, send = halves(total, bit)
            got = yield [dp_swap(send, bit)]
            total = (keep.astype(F32) + got[0].astype(F32)).astype(BF16)
        for bit in reversed(range(bits)):
            at = (d_idx >> bit) & 1
            got = yield [dp_swap(total, bit)]
            total = jnp.where(
                at == 0,
                jnp.concatenate([total, got[0]], 0),
                jnp.concatenate([got[0], total], 0),
            )
        return total.astype(F32)

    def begin(blocks, dp_first=False):
        flow = reduce_blocks(blocks, dp_first)
        return [flow, next(flow)]

    def advance(flow, got):
        flow[1] = flow[0].send(got)

    def finish(flow):
        try:
            while True:
                advance(flow, flow[1])
        except StopIteration as end:
            return end.value

    def tie(value, *flows):
        value, arrived = lax.optimization_barrier((value, [flow[1] for flow in flows]))
        for flow, got in zip(flows, arrived):
            advance(flow, got)
        return value

    def after(value, *earlier):
        return lax.optimization_barrier((value, earlier))[0]

    gain_one, shift_one = ln1_gain.astype(F32), ln1_bias.astype(F32)
    gain_two, shift_two = ln2_gain.astype(F32), ln2_bias.astype(F32)

    x_got = fetch_rows(inputs)
    cat_qkv = jnp.concatenate([w_qkv[n] for n in range(3)], axis=1)
    q_got = fetch_weight(cat_qkv)
    small = jnp.concatenate([bias_up, bias_qv.reshape(-1)])
    small_got = [chip_shift(small, step) for step in steps]
    o_got = fetch_weight(w_out)
    u_got = fetch_weight(w_up)
    dy_got = fetch_rows(cotangent)
    d_got = fetch_weight(w_down)

    n_up = bias_up.shape[0]
    scale = jnp.concatenate([jnp.full((width,), 0.125, F32), jnp.ones((2 * width,), F32)])

    def qkv_bias(vector):
        vector = vector[n_up:].astype(F32)
        return jnp.concatenate([vector[:width], jnp.zeros((width,), F32), vector[width:]])

    def project(block, vector):
        return ((mm(normed_one, block, NN) + qkv_bias(vector)) * scale).astype(BF16)

    x32 = core_rows(inputs, x_got).astype(F32)
    mean_one, inv_one = norm_stats(x32)
    unit_one = (x32 - mean_one) * inv_one
    normed_one = complete((unit_one * gain_one + shift_one).astype(BF16))
    qkv = [project(cat_qkv, small)]
    qkv[0], q_got = lax.optimization_barrier((qkv[0], q_got))
    wq = whole_weight(cat_qkv, q_got)
    o, lse = attention_forward(qkv[0], images, seq)
    o, o_got, small_got = lax.optimization_barrier((o, o_got, small_got))
    heads, norms = [o], [lse]
    wo = whole_weight(w_out, o_got)
    smalls = [small] + small_got
    for r in steps:
        qkv.append(project(wq[r], smalls[r]))
        o, lse = attention_forward(qkv[r], images, seq)
        heads.append(o)
        norms.append(lse)
    heads[-1], u_got = lax.optimization_barrier((heads[-1], u_got))
    wu = whole_weight(w_up, u_got)
    attn_part = mm(heads[0], wo[0], NN)
    for r in steps:
        attn_part = attn_part + mm(heads[r], wo[r], NN)
    resid = x32 + (exchange(attn_part) + bias_out.astype(F32))
    mean_two, inv_two = norm_stats(resid)
    unit_two = (resid - mean_two) * inv_two
    normed_two = complete((unit_two * gain_two + shift_two).astype(BF16))
    normed_two, dy_got = lax.optimization_barrier((normed_two, dy_got))

    acts, slopes = [], []
    for r in range(chips):
        hidden = mm(normed_two, wu[r], NN) + smalls[r][:n_up].astype(F32)
        sigma = jax.nn.sigmoid(GELU_K * hidden)
        acts.append((hidden * sigma).astype(BF16))
        slopes.append(sigma + GELU_K * hidden * sigma * (1.0 - sigma))
    acts[-1], d_got = lax.optimization_barrier((acts[-1], d_got))
    wd = whole_weight(w_down, d_got)

    live = my_images(slot_mask, 0).astype(BF16)
    if split:
        live = by_core(live[:near], live[near:])
    dy_local = core_rows(cotangent, dy_got).reshape(near, padded, full)
    dy_local = (dy_local * live[:, None, None]).reshape(local, full)
    dy = complete(dy_local)
    down_blocks = [None] + [mm(acts[r], dy, TN).astype(BF16) for r in steps]
    down_blocks[0] = mm(after(acts[0], *down_blocks[1:]), dy, TN).astype(BF16)
    flow_down = begin(down_blocks)
    d_hidden = [(mm(dy, wd[r], NT) * slopes[r]).astype(BF16) for r in range(chips)]
    up_blocks = [None] + [mm(normed_two, d_hidden[r], TN).astype(BF16) for r in steps]
    up_blocks[0] = mm(normed_two, after(d_hidden[0], *up_blocks[1:]), TN).astype(BF16)
    flow_up = begin(up_blocks)
    part_two = mm(d_hidden[0], wu[0], NT)
    for r in steps:
        part_two = part_two + mm(d_hidden[r], wu[r], NT)
    back_two, g_gain_two, g_shift_two = norm_back(exchange(part_two), unit_two, inv_two, gain_two)
    d_resid = dy_local.astype(F32) + back_two
    da_local = d_resid.astype(BF16)
    da = tie(complete(da_local), flow_down)

    grads = [None] * chips
    last = da
    for r in list(steps) + [0]:
        do = mm(last, wo[r], NT).astype(BF16)
        grads[r] = attention_backward(qkv[r], do, norms[r], images, seq)
        if r:
            grads[r] = tie(grads[r], flow_down)
            last = after(da, grads[r])
    grads[0] = tie(grads[0], flow_down, flow_up)
    out_blocks = [mm(heads[r], da, TN).astype(BF16) for r in range(chips)]
    flow_out = begin(out_blocks)
    qkv_blocks = [None] + [mm(normed_one, grads[r], TN).astype(BF16) for r in steps]
    qkv_blocks[0] = mm(normed_one, grads[0], TN).astype(BF16)
    middle = full // 2
    flow_low = begin([block[:middle] for block in qkv_blocks])
    flow_high = begin([block[middle:] for block in qkv_blocks], True)
    part_one = mm(grads[0], wq[0], NT)
    for r in steps:
        part_one = part_one + mm(grads[r], wq[r], NT)
    back_one, g_gain_one, g_shift_one = norm_back(exchange(part_one), unit_one, inv_one, gain_one)
    input_grad = scatter_rows((d_resid + back_one).astype(BF16))

    mlp_part = mm(after(acts[0], grads[0]), wd[0], NN)
    for r in steps:
        mlp_part = mlp_part + mm(acts[r], wd[r], NN)
    out = (resid + (exchange(mlp_part) + bias_down.astype(F32))).astype(BF16)
    layer_out = scatter_rows(out)

    shared = jnp.concatenate(
        [
            jnp.sum(da_local, axis=0, dtype=F32),
            g_gain_one,
            g_shift_one,
            g_gain_two,
            g_shift_two,
            jnp.sum(dy_local, axis=0, dtype=F32),
        ]
    )
    if split:
        shared = shared + core_swap(shared)
    own = []
    for r in range(chips):
        rows_sum = jnp.sum(grads[r], axis=0, dtype=F32)
        own.append(
            jnp.concatenate(
                [
                    shared,
                    jnp.sum(d_hidden[r], axis=0, dtype=F32),
                    rows_sum[:width],
                    rows_sum[2 * width :],
                ]
            )
        )
    vector = own[0]
    for step in steps:
        vector = vector + chip_shift(own[step], chips - step)
    for bit in range(bits):
        vector = vector + dp_swap(vector, bit)
    vecs = [vector[n * full : (n + 1) * full] for n in range(6)]
    mine = vector[6 * full :]

    grad_down = finish(flow_down)
    grad_up = finish(flow_up)
    grad_out = finish(flow_out)
    grad_cat = jnp.concatenate([finish(flow_low), finish(flow_high)], axis=0)
    grad_qkv = jnp.stack([grad_cat[:, n * width : (n + 1) * width] for n in range(3)])
    return (
        layer_out,
        input_grad,
        grad_qkv,
        mine[n_up:].reshape(2, width),
        grad_out,
        vecs[0],
        vecs[1],
        vecs[2],
        vecs[3],
        vecs[4],
        grad_up,
        mine[:n_up],
        grad_down,
        vecs[5],
    )


def solution(mesh):
    return jax.shard_map(
        per_device,
        mesh=mesh,
        in_specs=(
            P("dp", None, "tensor"),
            P("dp", None, "tensor"),
            P("dp"),
            P(None, None, "tensor"),
            P(None, "tensor"),
            P("tensor", None),
            P(),
            P(),
            P(),
            P(),
            P(),
            P(None, "tensor"),
            P("tensor"),
            P("tensor", None),
            P(),
        ),
        out_specs=(
            P("dp", None, "tensor"),
            P("dp", None, "tensor"),
            P(None, None, "tensor"),
            P(None, "tensor"),
            P("tensor", None),
            P(),
            P(),
            P(),
            P(),
            P(),
            P(None, "tensor"),
            P("tensor"),
            P("tensor", None),
            P(),
        ),
        check_vma=False,
    )
```

```python
import functools

import jax
import jax.numpy as jnp
from jax import lax
from jax.experimental import pallas as pl
from jax.experimental.pallas import tpu as pltpu
from jax.sharding import PartitionSpec as P

HEAD = 64
LANES = 128
ROW_TILE = 16
EPS = 1e-05
GELU_K = 1.702
FAR = -1e30

F32 = jnp.float32
BF16 = jnp.bfloat16

NT = (((1,), (1,)), ((), ()))
NN = (((1,), (0,)), ((), ()))
TN = (((0,), (0,)), ((), ()))


def mm(left, right, dims):
    return lax.dot_general(left, right, dims, preferred_element_type=F32)


def head_views(half, seq, q, k):
    lane = lax.broadcasted_iota(jnp.int32, q.shape, 1)
    row = lax.broadcasted_iota(jnp.int32, q.shape, 0)
    mine = (lane >= HEAD) if half else (lane < HEAD)
    spare = lane == (0 if half else HEAD)
    zero = jnp.zeros_like(q)
    q_only = jnp.where(mine, q, zero)
    k_only = jnp.where(mine, k, zero)
    q_mask = jnp.where(spare, jnp.ones_like(q), q_only)
    far = jnp.full_like(k, FAR)
    k_mask = jnp.where(spare & (row >= seq), far, k_only)
    return mine, q_only, k_only, q_mask, k_mask


def attn_fwd_kernel(seq, q_ref, k_ref, v_ref, o_ref, lse_ref):
    q, k, v = q_ref[...], k_ref[...], v_ref[...]
    v_t = v.T
    pieces = []
    for half in range(2):
        _, _, _, q_mask, k_mask = head_views(half, seq, q, k)
        s_t = mm(k_mask, q_mask, NT)
        peak = jnp.max(s_t, axis=0, keepdims=True)
        expo = jnp.exp(s_t - peak)
        total = jnp.sum(expo, axis=0, keepdims=True)
        p_t = (expo * (1.0 / total)).astype(BF16)
        pieces.append(mm(v_t[half * HEAD : (half + 1) * HEAD], p_t, NN))
        lse_ref[0, 0, half : half + 1, :] = peak + jnp.log(total)
    o_ref[...] = jnp.concatenate(pieces, axis=0).T.astype(BF16)


def attn_bwd_kernel(seq, width, q_ref, k_ref, v_ref, do_ref, lse_ref, grads_ref):
    q, k, v, do = q_ref[...], k_ref[...], v_ref[...], do_ref[...]
    k_t = k.T
    dq_t, dk, dv = [], None, None
    for half in range(2):
        mine, q_only, _, q_mask, k_mask = head_views(half, seq, q, k)
        do_only = jnp.where(mine, do, jnp.zeros_like(do))
        s_t = mm(k_mask, q_mask, NT)
        p_t = jnp.exp(s_t - lse_ref[0, 0, half : half + 1, :])
        dp_t = mm(v, do_only, NT)
        inner = jnp.sum(p_t * dp_t, axis=0, keepdims=True)
        ds_t = (p_t * (dp_t - inner)).astype(BF16)
        dv_half = mm(p_t.astype(BF16), do_only, NN)
        dk_half = mm(ds_t, q_only, NN)
        dq_t.append(mm(k_t[half * HEAD : (half + 1) * HEAD], ds_t, NN))
        dv = dv_half if dv is None else dv + dv_half
        dk = dk_half if dk is None else dk + dk_half
    dq = jnp.concatenate(dq_t, axis=0).T.astype(BF16) * 0.125
    for n, grad in enumerate((dq, dk.astype(BF16), dv.astype(BF16))):
        at = pl.multiple_of(n * width + pl.program_id(1) * LANES, LANES)
        grads_ref[:, pl.ds(at, LANES)] = grad


def column_blocks(s, pairs, parts):
    def at(part):
        return pl.BlockSpec((s, LANES), lambda i, j: (i, part * pairs + j))

    return [at(part) for part in range(parts)]


def attention_forward(qkv, images, seq):
    rows, width = qkv.shape[0], qkv.shape[1] // 3
    s = rows // images
    pairs = width // LANES
    block = pl.BlockSpec((s, LANES), lambda i, j: (i, j))
    lse_block = pl.BlockSpec((1, 1, 2, s), lambda i, j: (i, j, 0, 0))
    n = images * pairs * 2
    return pl.pallas_call(
        functools.partial(attn_fwd_kernel, seq),
        grid=(images, pairs),
        in_specs=column_blocks(s, pairs, 3),
        out_specs=[block, lse_block],
        out_shape=[
            jax.ShapeDtypeStruct((rows, width), BF16),
            jax.ShapeDtypeStruct((images, pairs, 2, s), F32),
        ],
        cost_estimate=pl.CostEstimate(
            flops=n * 4 * s * s * 256, bytes_accessed=rows * width * 8, transcendentals=n * s * s
        ),
        name="attn_fwd",
    )(qkv, qkv, qkv)


def attention_backward(qkv, do, lse, images, seq):
    rows, width = do.shape
    s = rows // images
    pairs = width // LANES
    block = pl.BlockSpec((s, LANES), lambda i, j: (i, j))
    lse_block = pl.BlockSpec((1, 1, 2, s), lambda i, j: (i, j, 0, 0))
    n = images * pairs * 2
    return pl.pallas_call(
        functools.partial(attn_bwd_kernel, seq, width),
        grid=(images, pairs),
        in_specs=column_blocks(s, pairs, 3) + [block, lse_block],
        out_specs=pl.BlockSpec((s, 3 * width), lambda i, j: (i, 0)),
        out_shape=jax.ShapeDtypeStruct((rows, 3 * width), BF16),
        cost_estimate=pl.CostEstimate(
            flops=n * 10 * s * s * 256, bytes_accessed=rows * width * 14, transcendentals=n * s * s
        ),
        name="attn_bwd",
    )(qkv, qkv, qkv, do, lse)


def norm_stats(rows):
    mean = jnp.mean(rows, axis=-1, keepdims=True)
    center = rows - mean
    inv = lax.rsqrt(jnp.mean(center * center, axis=-1, keepdims=True) + EPS)
    return mean, inv


def norm_back(grad, unit, inv, gain):
    scaled = grad * gain
    first = jnp.mean(scaled, axis=-1, keepdims=True)
    second = jnp.mean(scaled * unit, axis=-1, keepdims=True)
    return (
        inv * (scaled - first - unit * second),
        jnp.sum(grad * unit, axis=0),
        jnp.sum(grad, axis=0),
    )


def pick(pieces, index):
    out = pieces[0]
    for n in range(1, len(pieces)):
        out = jnp.where(index == n, pieces[n], out)
    return out


def per_device(
    inputs,
    cotangent,
    slot_mask,
    w_qkv,
    bias_qv,
    w_out,
    bias_out,
    ln1_gain,
    ln1_bias,
    ln2_gain,
    ln2_bias,
    w_up,
    bias_up,
    w_down,
    bias_down,
):
    n_img, seq, width = inputs.shape
    n_tensor = lax.axis_size("tensor")
    n_dp = lax.axis_size("dp")
    chips = n_tensor // 2
    images = n_img // chips
    full = width * n_tensor
    padded = -(-seq // ROW_TILE) * ROW_TILE
    split = images % 2 == 0
    near = images // 2 if split else images
    local = near * padded
    t_idx = lax.axis_index("tensor")
    d_idx = lax.axis_index("dp")
    chip, core = t_idx // 2, t_idx % 2
    bits = n_dp.bit_length() - 1
    side = d_idx & 1
    steps = range(1, chips)

    def chip_shift(value, step):
        perm = [
            (2 * a + b, 2 * ((a + step) % chips) + b) for a in range(chips) for b in range(2)
        ]
        return lax.ppermute(value, "tensor", perm)

    def core_swap(value):
        return lax.ppermute(value, "tensor", [(a, a ^ 1) for a in range(n_tensor)])

    def core_trade(value):
        pairs = [[2 * a, 2 * a + 1] for a in range(chips)]
        return lax.all_to_all(value, "tensor", 0, 0, axis_index_groups=pairs)

    def dp_swap(value, bit):
        return lax.ppermute(value, "dp", [(a, a ^ (1 << bit)) for a in range(n_dp)])

    def my_images(value, step):
        return lax.dynamic_slice_in_dim(value, ((chip + step) % chips) * images, images, 0)

    def by_core(first, second):
        return jnp.where(core == 0, first, second)

    def fetch_rows(value):
        return [chip_shift(my_images(value, step), step) for step in steps]

    def core_rows(value, arrived, whole):
        mine = jnp.concatenate([my_images(value, 0)] + arrived, axis=2)
        if split and not whole:
            both = core_trade(mine.reshape(2, near, seq, chips * width))
            both = [both[0], both[1]]
        else:
            got = core_swap(mine)
            both = [by_core(mine, got), by_core(got, mine)]
        both = [[b[:, :, a * width : (a + 1) * width] for a in range(chips)] for b in both]
        parts = []
        for a in range(chips):
            parts += [pick(b, (chip - a) % chips) for b in both]
        out = jnp.concatenate(parts, axis=2)
        out = jnp.pad(out, ((0, 0), (0, padded - seq), (0, 0)))
        return out.reshape(-1, full)

    def complete(rows):
        if split:
            rows = core_trade(jnp.broadcast_to(rows, (2,) + rows.shape)).reshape(-1, full)
        return rows

    def exchange(part):
        part = part.astype(BF16)
        if split:
            both = core_trade(part.reshape(2, local, full)).astype(F32)
            return both[0] + both[1]
        return part.astype(F32) + core_swap(part).astype(F32)

    def own_columns(value):
        value = value.reshape(near, padded, full)[:, :seq]
        cols = [value[:, :, n * width : (n + 1) * width] for n in range(n_tensor)]
        cols = [jnp.concatenate(cols[core_of::2], axis=2) for core_of in range(2)]
        if split:
            keep = core_trade(jnp.stack(cols)).reshape(images, seq, chips * width)
        else:
            keep = by_core(*cols)
        return [keep[:, :, a * width : (a + 1) * width] for a in range(chips)]

    def scatter_rows(keep):
        pieces = [pick(keep, chip)]
        for step in steps:
            pieces.append(chip_shift(pick(keep, (chip + step) % chips), step))
        return jnp.concatenate([pick(pieces, (chip - a) % chips) for a in range(chips)], axis=0)

    def my_half(weight):
        half = weight.shape[0] // 2
        return lax.dynamic_slice_in_dim(weight, side * half, half, 0)

    def fetch(send):
        return [chip_shift(send, step) for step in steps]

    def other_halves(arrived):
        return [dp_swap(got, 0) for got in arrived]

    def whole_weight(weight, arrived, others):
        blocks = [weight]
        for got, other in zip(arrived, others):
            block = jnp.where(
                side == 0,
                jnp.concatenate([got, other], 0),
                jnp.concatenate([other, got], 0),
            )
            blocks.append(lax.optimization_barrier(block))
        return blocks

    def halves(value, bit):
        half = value.shape[0] // 2
        at = (d_idx >> bit) & 1
        keep = lax.dynamic_slice_in_dim(value, at * half, half, 0)
        send = lax.dynamic_slice_in_dim(value, (1 - at) * half, half, 0)
        return keep, send

    def add(left, right):
        return (left.astype(F32) + right.astype(F32)).astype(BF16)

    def reduce_blocks(blocks, dp_first):
        first = 0
        if dp_first:
            cut = [halves(block, 0) for block in blocks]
            send = yield [jnp.concatenate([c[1] for c in cut], 0)]
            got = dp_swap(send[0], 0)
            size = cut[0][0].shape[0]
            blocks = [add(c[0], got[n * size : (n + 1) * size]) for n, c in enumerate(cut)]
            first = 1
        send = yield blocks[1:]
        total = blocks[0].astype(F32)
        for step in steps:
            total = total + chip_shift(send[step - 1], chips - step).astype(F32)
        total = total.astype(BF16)
        for bit in range(first, bits - 1):
            keep, send = halves(total, bit)
            send = yield [send]
            total = add(keep, dp_swap(send[0], bit))
        send = yield [total]
        total = add(total, dp_swap(send[0], bits - 1))
        for bit in reversed(range(bits - 1)):
            at = (d_idx >> bit) & 1
            send = yield [total]
            got = dp_swap(send[0], bit)
            total = jnp.where(
                at == 0,
                jnp.concatenate([total, got], 0),
                jnp.concatenate([got, total], 0),
            )
        return total.astype(F32)

    def begin(blocks, dp_first=False):
        flow = reduce_blocks(blocks, dp_first)
        return [flow, next(flow), None]

    def tie(value, *flows):
        flows = [flow for flow in flows if flow[2] is None]
        value, sends = lax.optimization_barrier((value, [flow[1] for flow in flows]))
        for flow, send in zip(flows, sends):
            advance(flow, send)
        return value

    def advance(flow, send):
        try:
            flow[1] = flow[0].send(send)
        except StopIteration as end:
            flow[1:] = [], end.value

    def finish(flow):
        while flow[2] is None:
            advance(flow, flow[1])
        return flow[2]

    def hold(*values):
        return lax.optimization_barrier(values)

    def after(value, *earlier):
        return lax.optimization_barrier((value, earlier))[0]

    gain_one, shift_one = ln1_gain.astype(F32), ln1_bias.astype(F32)
    gain_two, shift_two = ln2_gain.astype(F32), ln2_bias.astype(F32)

    n_up = bias_up.shape[0]
    small = jnp.concatenate([bias_up, bias_qv.reshape(-1)])
    spare = -small.shape[0] % (ROW_TILE * full)
    small_rows = jnp.pad(small, (0, spare)).reshape(-1, full)
    x_got = fetch_rows(inputs)
    cat_qkv = jnp.concatenate([w_qkv[n] for n in range(3)], axis=1)
    out_rows = jnp.concatenate([my_half(w_out), small_rows], axis=0)
    sends = [my_half(cat_qkv), out_rows, my_half(w_up), my_half(w_down)]
    dy_sends = [my_images(cotangent, step) for step in steps]
    x_got, sends, dy_sends = hold(x_got, sends, dy_sends)
    q_got, o_got, u_got = [fetch(send) for send in sends[:3]]
    scale = jnp.concatenate([jnp.full((width,), 0.125, F32), jnp.ones((2 * width,), F32)])

    def qkv_bias(vector):
        vector = vector[n_up:].astype(F32)
        return jnp.concatenate([vector[:width], jnp.zeros((width,), F32), vector[width:]])

    def project(block, vector):
        return ((mm(normed_one, block, NN) + qkv_bias(vector)) * scale).astype(BF16)

    x32 = core_rows(inputs, x_got, False).astype(F32)
    mean_one, inv_one = norm_stats(x32)
    unit_one = (x32 - mean_one) * inv_one
    normed_one = complete((unit_one * gain_one + shift_one).astype(BF16))
    qkv = [project(cat_qkv, small)]
    qkv[0], q_got = hold(qkv[0], q_got)
    q_more = other_halves(q_got)
    o, lse = attention_forward(qkv[0], images, seq)
    heads, norms = [o], [lse]
    q_more, o_got = hold(q_more, o_got)
    half_out = w_out.shape[0] // 2
    smalls = [small] + [got[half_out:].reshape(-1)[: small.shape[0]] for got in o_got]
    o_got = [got[:half_out] for got in o_got]
    o_more = other_halves(o_got)
    wq = whole_weight(cat_qkv, q_got, q_more)
    for r in steps:
        qkv.append(project(wq[r], smalls[r]))
    qkv[-1], dy_sends, d_send = hold(qkv[-1], dy_sends, sends[3])
    dy_got = [chip_shift(send, step) for step, send in zip(steps, dy_sends)]
    d_got = fetch(d_send)
    for r in steps:
        o, lse = attention_forward(qkv[r], images, seq)
        heads.append(o)
        norms.append(lse)
    heads[-1], u_got, o_more = hold(heads[-1], u_got, o_more)
    u_more = other_halves(u_got)
    wo = whole_weight(w_out, o_got, o_more)
    attn_part = mm(heads[0], wo[0], NN)
    for r in steps:
        attn_part = attn_part + mm(heads[r], wo[r], NN)
    resid = x32 + (exchange(attn_part) + bias_out.astype(F32))
    mean_two, inv_two = norm_stats(resid)
    unit_two = (resid - mean_two) * inv_two
    normed_two = complete((unit_two * gain_two + shift_two).astype(BF16))
    normed_two, dy_got, u_more = hold(normed_two, dy_got, u_more)

    live = my_images(slot_mask, 0).astype(BF16)
    dy = core_rows(cotangent, dy_got, True).reshape(images, padded, full)
    dy = (dy * live[:, None, None]).reshape(-1, full)
    dy_local = lax.dynamic_slice_in_dim(dy, core * local, local, 0) if split else dy
    acts, slopes = [], []

    def hidden_units(rows, block, vector):
        hidden = mm(rows, block, NN) + vector[:n_up].astype(F32)
        sigma = jax.nn.sigmoid(GELU_K * hidden)
        acts.append((hidden * sigma).astype(BF16))
        slopes.append(sigma + GELU_K * hidden * sigma * (1.0 - sigma))

    hidden_units(normed_two, w_up, small)
    acts[0], dy, d_got = hold(acts[0], dy, d_got)
    d_more = other_halves(d_got)
    wu = whole_weight(w_up, u_got, u_more)
    for r in steps:
        hidden_units(normed_two, wu[r], smalls[r])

    down_sent = [mm(acts[r], dy, TN).astype(BF16) for r in steps]
    first_act, dy, down_sent = lax.optimization_barrier((acts[0], dy, down_sent))
    down_blocks = [mm(first_act, dy, TN).astype(BF16)] + down_sent
    d_hidden = [(mm(dy, w_down, NT) * slopes[0]).astype(BF16)]
    up_blocks = [mm(normed_two, d_hidden[0], TN).astype(BF16)]
    up_blocks[0], d_more = lax.optimization_barrier((up_blocks[0], d_more))
    wd = whole_weight(w_down, d_got, d_more)
    for r in steps:
        d_hidden.append((mm(dy, wd[r], NT) * slopes[r]).astype(BF16))
        up_blocks.append(mm(normed_two, d_hidden[r], TN).astype(BF16))
    d_hidden, up_blocks = lax.optimization_barrier((d_hidden, up_blocks))
    flow_down = begin(down_blocks)
    flow_up = begin(up_blocks)
    flow_down[1] = flow_down[0].send(flow_down[1])
    flow_up[1] = flow_up[0].send(flow_up[1])
    part_two = mm(d_hidden[0], wu[0], NT)
    for r in steps:
        part_two = part_two + mm(d_hidden[r], wu[r], NT)
    back_two, g_gain_two, g_shift_two = norm_back(exchange(part_two), unit_two, inv_two, gain_two)
    d_resid = dy_local.astype(F32) + back_two
    da_local = d_resid.astype(BF16)
    da = tie(complete(da_local), flow_down)

    middle = full // 2
    grads, lows, highs = [None] * chips, [None] * chips, [None] * chips
    part_one = None
    last = da
    for r in list(steps) + [0]:
        do = mm(last, wo[r], NT).astype(BF16)
        grads[r] = attention_backward(qkv[r], do, norms[r], images, seq)
        if r == chips - 1:
            grads[r] = tie(grads[r], flow_down)
        if r == 0:
            grads[r] = tie(grads[r], flow_down, flow_up)
        of_qkv = mm(normed_one, grads[r], TN).astype(BF16)
        of_out = mm(da, heads[r], TN).astype(BF16)
        lows[r] = jnp.concatenate([of_qkv[:middle], of_out[:middle]], axis=1)
        highs[r] = jnp.concatenate([of_qkv[middle:], of_out[middle:]], axis=1)
        part = mm(grads[r], wq[r], NT)
        part_one = part if part_one is None else part_one + part
        if r:
            last, lows[r], highs[r] = lax.optimization_barrier((last, lows[r], highs[r]))
            if r == chips - 1:
                last = tie(last, flow_down)
    flow_low = begin(lows)
    flow_low[1] = flow_low[0].send(flow_low[1])
    flow_high = begin(highs)
    flow_high[1] = flow_high[0].send(flow_high[1])
    back_one, g_gain_one, g_shift_one = norm_back(exchange(part_one), unit_one, inv_one, gain_one)
    input_rows = tie((d_resid + back_one).astype(BF16), flow_up, flow_low)

    def reduce_small():
        shared = jnp.concatenate(
            [
                jnp.sum(da_local, axis=0, dtype=F32),
                g_gain_one,
                g_shift_one,
                g_gain_two,
                g_shift_two,
                jnp.sum(dy_local, axis=0, dtype=F32),
            ]
        )
        if split:
            send = yield shared
            shared = shared + core_swap(send)
        own = []
        for r in range(chips):
            rows_sum = jnp.sum(grads[r], axis=0, dtype=F32)
            hidden_sum = jnp.sum(d_hidden[r], axis=0, dtype=F32)
            own.append(
                jnp.concatenate([shared, hidden_sum, rows_sum[:width], rows_sum[2 * width :]])
            )
        send = yield own[1:]
        vector = own[0]
        for step in steps:
            vector = vector + chip_shift(send[step - 1], chips - step)
        for bit in list(range(1, bits)) + [0]:
            send = yield vector
            vector = vector + dp_swap(send, bit)
        return vector

    flow_small = reduce_small()
    flow_small = [flow_small, next(flow_small), None]

    mlp_part = mm(after(acts[0], input_rows), w_down, NN)
    for r in steps:
        mlp_part = mlp_part + mm(acts[r], wd[r], NN)
    mlp_part = tie(mlp_part, flow_small, flow_high, flow_down, flow_up)
    out = (resid + (exchange(mlp_part) + bias_down.astype(F32))).astype(BF16)
    out = tie(out, flow_small, flow_low)
    keep = [
        jnp.concatenate(pair, axis=2) for pair in zip(own_columns(out), own_columns(input_rows))
    ]
    both = scatter_rows(keep)
    layer_out, input_grad = both[:, :, :width], both[:, :, width:]

    token = after(slot_mask, keep)
    for flow in (
        flow_high,
        flow_low,
        flow_small,
        flow_up,
        flow_high,
        flow_small,
        flow_up,
        flow_low,
        flow_high,
        flow_low,
        flow_small,
        flow_high,
    ):
        token = tie(token, flow)
    vector = finish(flow_small)
    vecs = [vector[n * full : (n + 1) * full] for n in range(6)]
    mine = vector[6 * full :]

    grad_down = finish(flow_down)
    grad_up = finish(flow_up)
    grad_cat = jnp.concatenate([finish(flow_low), finish(flow_high)], axis=0)
    grad_qkv = jnp.stack([grad_cat[:, n * width : (n + 1) * width] for n in range(3)])
    grad_out = grad_cat[:, 3 * width :].T
    return (
        layer_out,
        input_grad,
        grad_qkv,
        mine[n_up:].reshape(2, width),
        grad_out,
        vecs[0],
        vecs[1],
        vecs[2],
        vecs[3],
        vecs[4],
        grad_up,
        mine[:n_up],
        grad_down,
        vecs[5],
    )


def solution(mesh):
    return jax.shard_map(
        per_device,
        mesh=mesh,
        in_specs=(
            P("dp", None, "tensor"),
            P("dp", None, "tensor"),
            P("dp"),
            P(None, None, "tensor"),
            P(None, "tensor"),
            P("tensor", None),
            P(),
            P(),
            P(),
            P(),
            P(),
            P(None, "tensor"),
            P("tensor"),
            P("tensor", None),
            P(),
        ),
        out_specs=(
            P("dp", None, "tensor"),
            P("dp", None, "tensor"),
            P(None, None, "tensor"),
            P(None, "tensor"),
            P("tensor", None),
            P(),
            P(),
            P(),
            P(),
            P(),
            P(None, "tensor"),
            P("tensor"),
            P("tensor", None),
            P(),
        ),
        check_vma=False,
    )
```

```python
import functools

import jax
import jax.numpy as jnp
from jax import lax
from jax.experimental import pallas as pl
from jax.experimental.pallas import tpu as pltpu
from jax.sharding import PartitionSpec as P

HEAD = 64
LANES = 128
ROW_TILE = 16
EPS = 1e-05
GELU_K = 1.702
FAR = -1e30

F32 = jnp.float32
BF16 = jnp.bfloat16

NT = (((1,), (1,)), ((), ()))
NN = (((1,), (0,)), ((), ()))
TN = (((0,), (0,)), ((), ()))


def mm(left, right, dims):
    return lax.dot_general(left, right, dims, preferred_element_type=F32)


def head_views(half, seq, q, k):
    lane = lax.broadcasted_iota(jnp.int32, q.shape, 1)
    row = lax.broadcasted_iota(jnp.int32, q.shape, 0)
    mine = (lane >= HEAD) if half else (lane < HEAD)
    spare = lane == (0 if half else HEAD)
    zero = jnp.zeros_like(q)
    q_only = jnp.where(mine, q, zero)
    k_only = jnp.where(mine, k, zero)
    q_mask = jnp.where(spare, jnp.ones_like(q), q_only)
    far = jnp.full_like(k, FAR)
    k_mask = jnp.where(spare & (row >= seq), far, k_only)
    return mine, q_only, k_only, q_mask, k_mask


def attn_fwd_kernel(seq, q_ref, k_ref, v_ref, o_ref, lse_ref):
    q, k, v = q_ref[...], k_ref[...], v_ref[...]
    v_t = v.T
    pieces = []
    for half in range(2):
        _, _, _, q_mask, k_mask = head_views(half, seq, q, k)
        s_t = mm(k_mask, q_mask, NT)
        peak = jnp.max(s_t, axis=0, keepdims=True)
        expo = jnp.exp(s_t - peak)
        total = jnp.sum(expo, axis=0, keepdims=True)
        p_t = (expo * (1.0 / total)).astype(BF16)
        pieces.append(mm(v_t[half * HEAD : (half + 1) * HEAD], p_t, NN))
        lse_ref[0, 0, half : half + 1, :] = peak + jnp.log(total)
    o_ref[...] = jnp.concatenate(pieces, axis=0).T.astype(BF16)


def attn_bwd_kernel(seq, width, q_ref, k_ref, v_ref, do_ref, lse_ref, grads_ref):
    q, k, v, do = q_ref[...], k_ref[...], v_ref[...], do_ref[...]
    k_t = k.T
    dq_t, dk, dv = [], None, None
    for half in range(2):
        mine, q_only, _, q_mask, k_mask = head_views(half, seq, q, k)
        do_only = jnp.where(mine, do, jnp.zeros_like(do))
        s_t = mm(k_mask, q_mask, NT)
        p_t = jnp.exp(s_t - lse_ref[0, 0, half : half + 1, :])
        dp_t = mm(v, do_only, NT)
        inner = jnp.sum(p_t * dp_t, axis=0, keepdims=True)
        ds_t = (p_t * (dp_t - inner)).astype(BF16)
        dv_half = mm(p_t.astype(BF16), do_only, NN)
        dk_half = mm(ds_t, q_only, NN)
        dq_t.append(mm(k_t[half * HEAD : (half + 1) * HEAD], ds_t, NN))
        dv = dv_half if dv is None else dv + dv_half
        dk = dk_half if dk is None else dk + dk_half
    dq = jnp.concatenate(dq_t, axis=0).T.astype(BF16) * 0.125
    for n, grad in enumerate((dq, dk.astype(BF16), dv.astype(BF16))):
        at = pl.multiple_of(n * width + pl.program_id(1) * LANES, LANES)
        grads_ref[:, pl.ds(at, LANES)] = grad


def column_blocks(s, pairs, parts):
    def at(part):
        return pl.BlockSpec((s, LANES), lambda i, j: (i, part * pairs + j))

    return [at(part) for part in range(parts)]


def attention_forward(qkv, images, seq):
    rows, width = qkv.shape[0], qkv.shape[1] // 3
    s = rows // images
    pairs = width // LANES
    block = pl.BlockSpec((s, LANES), lambda i, j: (i, j))
    lse_block = pl.BlockSpec((1, 1, 2, s), lambda i, j: (i, j, 0, 0))
    n = images * pairs * 2
    return pl.pallas_call(
        functools.partial(attn_fwd_kernel, seq),
        grid=(images, pairs),
        in_specs=column_blocks(s, pairs, 3),
        out_specs=[block, lse_block],
        out_shape=[
            jax.ShapeDtypeStruct((rows, width), BF16),
            jax.ShapeDtypeStruct((images, pairs, 2, s), F32),
        ],
        cost_estimate=pl.CostEstimate(
            flops=n * 4 * s * s * 256, bytes_accessed=rows * width * 8, transcendentals=n * s * s
        ),
        name="attn_fwd",
    )(qkv, qkv, qkv)


def attention_backward(qkv, do, lse, images, seq):
    rows, width = do.shape
    s = rows // images
    pairs = width // LANES
    block = pl.BlockSpec((s, LANES), lambda i, j: (i, j))
    lse_block = pl.BlockSpec((1, 1, 2, s), lambda i, j: (i, j, 0, 0))
    n = images * pairs * 2
    return pl.pallas_call(
        functools.partial(attn_bwd_kernel, seq, width),
        grid=(images, pairs),
        in_specs=column_blocks(s, pairs, 3) + [block, lse_block],
        out_specs=pl.BlockSpec((s, 3 * width), lambda i, j: (i, 0)),
        out_shape=jax.ShapeDtypeStruct((rows, 3 * width), BF16),
        cost_estimate=pl.CostEstimate(
            flops=n * 10 * s * s * 256, bytes_accessed=rows * width * 14, transcendentals=n * s * s
        ),
        name="attn_bwd",
    )(qkv, qkv, qkv, do, lse)


def norm_stats(rows):
    mean = jnp.mean(rows, axis=-1, keepdims=True)
    center = rows - mean
    inv = lax.rsqrt(jnp.mean(center * center, axis=-1, keepdims=True) + EPS)
    return mean, inv


def norm_back(grad, unit, inv, gain):
    scaled = grad * gain
    first = jnp.mean(scaled, axis=-1, keepdims=True)
    second = jnp.mean(scaled * unit, axis=-1, keepdims=True)
    return (
        inv * (scaled - first - unit * second),
        jnp.sum(grad * unit, axis=0),
        jnp.sum(grad, axis=0),
    )


def pick(pieces, index):
    out = pieces[0]
    for n in range(1, len(pieces)):
        out = jnp.where(index == n, pieces[n], out)
    return out


def per_device(
    inputs,
    cotangent,
    slot_mask,
    w_qkv,
    bias_qv,
    w_out,
    bias_out,
    ln1_gain,
    ln1_bias,
    ln2_gain,
    ln2_bias,
    w_up,
    bias_up,
    w_down,
    bias_down,
):
    n_img, seq, width = inputs.shape
    n_tensor = lax.axis_size("tensor")
    n_dp = lax.axis_size("dp")
    chips = n_tensor // 2
    images = n_img // chips
    full = width * n_tensor
    padded = -(-seq // ROW_TILE) * ROW_TILE
    split = images % 2 == 0
    near = images // 2 if split else images
    local = near * padded
    t_idx = lax.axis_index("tensor")
    d_idx = lax.axis_index("dp")
    chip, core = t_idx // 2, t_idx % 2
    bits = n_dp.bit_length() - 1
    side = d_idx & 1
    steps = range(1, chips)

    def chip_shift(value, step):
        perm = [
            (2 * a + b, 2 * ((a + step) % chips) + b) for a in range(chips) for b in range(2)
        ]
        return lax.ppermute(value, "tensor", perm)

    def core_swap(value):
        return lax.ppermute(value, "tensor", [(a, a ^ 1) for a in range(n_tensor)])

    def core_trade(value):
        pairs = [[2 * a, 2 * a + 1] for a in range(chips)]
        return lax.all_to_all(value, "tensor", 0, 0, axis_index_groups=pairs)

    def dp_swap(value, bit):
        return lax.ppermute(value, "dp", [(a, a ^ (1 << bit)) for a in range(n_dp)])

    def my_images(value, step):
        return lax.dynamic_slice_in_dim(value, ((chip + step) % chips) * images, images, 0)

    def by_core(first, second):
        return jnp.where(core == 0, first, second)

    def fetch_rows(value):
        return [chip_shift(my_images(value, step), step) for step in steps]

    def core_rows(value, arrived, whole):
        mine = jnp.concatenate([my_images(value, 0)] + arrived, axis=2)
        if split and not whole:
            got = core_swap(by_core(mine[near:], mine[:near]))
            mine = by_core(mine[:near], mine[near:])
        else:
            got = core_swap(mine)
        both = [by_core(mine, got), by_core(got, mine)]
        both = [[b[:, :, a * width : (a + 1) * width] for a in range(chips)] for b in both]
        parts = []
        for a in range(chips):
            parts += [pick(b, (chip - a) % chips) for b in both]
        out = jnp.concatenate(parts, axis=2)
        out = jnp.pad(out, ((0, 0), (0, padded - seq), (0, 0)))
        return out.reshape(-1, full)

    def complete(rows):
        if split:
            rows = core_trade(jnp.broadcast_to(rows, (2,) + rows.shape)).reshape(-1, full)
        return rows

    def exchange(part):
        part = part.astype(BF16)
        if split:
            both = core_trade(part.reshape(2, local, full)).astype(F32)
            return both[0] + both[1]
        return part.astype(F32) + core_swap(part).astype(F32)

    def own_columns(value):
        value = value.reshape(near, padded, full)[:, :seq]
        cols = [value[:, :, n * width : (n + 1) * width] for n in range(n_tensor)]
        cols = [jnp.concatenate(cols[core_of::2], axis=2) for core_of in range(2)]
        if split:
            keep = core_trade(jnp.stack(cols)).reshape(images, seq, chips * width)
        else:
            keep = by_core(*cols)
        return [keep[:, :, a * width : (a + 1) * width] for a in range(chips)]

    def scatter_rows(keep):
        pieces = [pick(keep, chip)]
        for step in steps:
            pieces.append(chip_shift(pick(keep, (chip + step) % chips), step))
        return jnp.concatenate([pick(pieces, (chip - a) % chips) for a in range(chips)], axis=0)

    def my_half(weight):
        half = weight.shape[0] // 2
        return lax.dynamic_slice_in_dim(weight, side * half, half, 0)

    def fetch(send):
        return [chip_shift(send, step) for step in steps]

    def other_halves(arrived):
        return [dp_swap(got, 0) for got in arrived]

    def whole_weight(weight, arrived, others):
        blocks = [weight]
        for got, other in zip(arrived, others):
            block = jnp.where(
                side == 0,
                jnp.concatenate([got, other], 0),
                jnp.concatenate([other, got], 0),
            )
            blocks.append(lax.optimization_barrier(block))
        return blocks

    def halves(value, bit):
        half = value.shape[0] // 2
        at = (d_idx >> bit) & 1
        keep = lax.dynamic_slice_in_dim(value, at * half, half, 0)
        send = lax.dynamic_slice_in_dim(value, (1 - at) * half, half, 0)
        return keep, send

    def add(left, right):
        return (left.astype(F32) + right.astype(F32)).astype(BF16)

    def reduce_blocks(blocks, dp_first):
        first = 0
        if dp_first:
            cut = [halves(block, 0) for block in blocks]
            send = yield [jnp.concatenate([c[1] for c in cut], 0)]
            got = dp_swap(send[0], 0)
            size = cut[0][0].shape[0]
            blocks = [add(c[0], got[n * size : (n + 1) * size]) for n, c in enumerate(cut)]
            first = 1
        send = yield blocks[1:]
        total = blocks[0].astype(F32)
        for step in steps:
            total = total + chip_shift(send[step - 1], chips - step).astype(F32)
        total = total.astype(BF16)
        for bit in range(first, bits - 1):
            keep, send = halves(total, bit)
            send = yield [send]
            total = add(keep, dp_swap(send[0], bit))
        send = yield [total]
        total = add(total, dp_swap(send[0], bits - 1))
        for bit in reversed(range(bits - 1)):
            at = (d_idx >> bit) & 1
            send = yield [total]
            got = dp_swap(send[0], bit)
            total = jnp.where(
                at == 0,
                jnp.concatenate([total, got], 0),
                jnp.concatenate([got, total], 0),
            )
        return total

    def begin(blocks, dp_first=False):
        flow = reduce_blocks(blocks, dp_first)
        return [flow, next(flow), None]

    def tie(value, *flows):
        flows = [flow for flow in flows if flow[2] is None]
        value, sends = lax.optimization_barrier((value, [flow[1] for flow in flows]))
        for flow, send in zip(flows, sends):
            advance(flow, send)
        return value

    def advance(flow, send):
        try:
            flow[1] = flow[0].send(send)
        except StopIteration as end:
            flow[1:] = [], end.value

    def finish(flow):
        while flow[2] is None:
            advance(flow, flow[1])
        return flow[2]

    def hold(*values):
        return lax.optimization_barrier(values)

    def after(value, *earlier):
        return lax.optimization_barrier((value, earlier))[0]

    gain_one, shift_one = ln1_gain.astype(F32), ln1_bias.astype(F32)
    gain_two, shift_two = ln2_gain.astype(F32), ln2_bias.astype(F32)

    n_up = bias_up.shape[0]
    small = jnp.concatenate([bias_up, bias_qv.reshape(-1)])
    spare = -small.shape[0] % (ROW_TILE * full)
    small_rows = jnp.pad(small, (0, spare)).reshape(-1, full)
    x_got = fetch_rows(inputs)
    cat_qkv = jnp.concatenate([w_qkv[n] for n in range(3)], axis=1)
    out_rows = jnp.concatenate([my_half(w_out), small_rows], axis=0)
    sends = [my_half(cat_qkv), out_rows, my_half(w_up), my_half(w_down)]
    dy_sends = [my_images(cotangent, step) for step in steps]
    x_got, sends, dy_sends = hold(x_got, sends, dy_sends)
    q_got, o_got, u_got = [fetch(send) for send in sends[:3]]
    scale = jnp.concatenate([jnp.full((width,), 0.125, F32), jnp.ones((2 * width,), F32)])

    def qkv_bias(vector):
        vector = vector[n_up:].astype(F32)
        return jnp.concatenate([vector[:width], jnp.zeros((width,), F32), vector[width:]])

    def project(block, vector):
        return ((mm(normed_one, block, NN) + qkv_bias(vector)) * scale).astype(BF16)

    x32 = core_rows(inputs, x_got, False).astype(F32)
    mean_one, inv_one = norm_stats(x32)
    unit_one = (x32 - mean_one) * inv_one
    normed_one = (unit_one * gain_one + shift_one).astype(BF16)
    normed_one = complete(normed_one)
    qkv = [project(cat_qkv, small)]
    qkv[0], q_got = hold(qkv[0], q_got)
    q_more = other_halves(q_got)
    o, lse = attention_forward(qkv[0], images, seq)
    heads, norms = [o], [lse]
    q_more, o_got = hold(q_more, o_got)
    half_out = w_out.shape[0] // 2
    smalls = [small] + [got[half_out:].reshape(-1)[: small.shape[0]] for got in o_got]
    o_got = [got[:half_out] for got in o_got]
    o_more = other_halves(o_got)
    wq = whole_weight(cat_qkv, q_got, q_more)
    for r in steps:
        qkv.append(project(wq[r], smalls[r]))
    qkv[-1], dy_sends, d_send = hold(qkv[-1], dy_sends, sends[3])
    dy_got = [chip_shift(send, step) for step, send in zip(steps, dy_sends)]
    d_got = fetch(d_send)
    for r in steps:
        o, lse = attention_forward(qkv[r], images, seq)
        heads.append(o)
        norms.append(lse)
    heads[-1], u_got, o_more = hold(heads[-1], u_got, o_more)
    u_more = other_halves(u_got)
    wo = whole_weight(w_out, o_got, o_more)
    attn_part = mm(heads[0], wo[0], NN)
    for r in steps:
        attn_part = attn_part + mm(heads[r], wo[r], NN)
    resid = x32 + (exchange(attn_part) + bias_out.astype(F32))
    mean_two, inv_two = norm_stats(resid)
    unit_two = (resid - mean_two) * inv_two
    normed_two = complete((unit_two * gain_two + shift_two).astype(BF16))
    normed_two, dy_got, u_more = hold(normed_two, dy_got, u_more)

    live = my_images(slot_mask, 0).astype(BF16)
    dy = core_rows(cotangent, dy_got, True).reshape(images, padded, full)
    dy = (dy * live[:, None, None]).reshape(-1, full)
    dy_local = lax.dynamic_slice_in_dim(dy, core * local, local, 0) if split else dy
    acts, slopes = [], []

    def hidden_units(rows, block, vector):
        hidden = mm(rows, block, NN) + vector[:n_up].astype(F32)
        sigma = jax.nn.sigmoid(GELU_K * hidden)
        acts.append((hidden * sigma).astype(BF16))
        slopes.append(sigma + GELU_K * hidden * sigma * (1.0 - sigma))

    hidden_units(normed_two, w_up, small)
    acts[0], dy, d_got = hold(acts[0], dy, d_got)
    d_more = other_halves(d_got)
    wu = whole_weight(w_up, u_got, u_more)
    for r in steps:
        hidden_units(normed_two, wu[r], smalls[r])

    down_sent = [mm(acts[r], dy, TN).astype(BF16) for r in steps]
    first_act, dy, down_sent = lax.optimization_barrier((acts[0], dy, down_sent))
    down_blocks = [mm(first_act, dy, TN).astype(BF16)] + down_sent
    d_hidden = [(mm(dy, w_down, NT) * slopes[0]).astype(BF16)]
    up_blocks = [mm(normed_two, d_hidden[0], TN).astype(BF16)]
    part_two = mm(d_hidden[0], w_up, NT)
    up_blocks[0], down_blocks[0], part_two, d_more = hold(
        up_blocks[0], down_blocks[0], part_two, d_more
    )
    wd = whole_weight(w_down, d_got, d_more)
    for r in steps:
        d_hidden.append((mm(dy, wd[r], NT) * slopes[r]).astype(BF16))
        up_blocks.append(mm(normed_two, d_hidden[r], TN).astype(BF16))
    d_hidden, up_blocks = lax.optimization_barrier((d_hidden, up_blocks))
    flow_down = begin(down_blocks)
    flow_up = begin(up_blocks)
    flow_down[1] = flow_down[0].send(flow_down[1])
    flow_up[1] = flow_up[0].send(flow_up[1])
    for r in steps:
        part_two = part_two + mm(d_hidden[r], wu[r], NT)
    back_two, g_gain_two, g_shift_two = norm_back(exchange(part_two), unit_two, inv_two, gain_two)
    d_resid = dy_local.astype(F32) + back_two
    da_local = d_resid.astype(BF16)
    da = tie(complete(da_local), flow_down)

    grads, attn_blocks = [None] * chips, [None] * chips
    part_one = None
    last = da
    for r in list(steps) + [0]:
        do = mm(last, wo[r], NT).astype(BF16)
        grads[r] = attention_backward(qkv[r], do, norms[r], images, seq)
        if r == chips - 1:
            grads[r] = tie(grads[r], flow_down)
        if r == 0:
            grads[r] = tie(grads[r], flow_up, flow_down)
        of_qkv = mm(normed_one, grads[r], TN).astype(BF16)
        of_out = mm(da, after(heads[r], grads[r]), TN).astype(BF16)
        attn_blocks[r] = jnp.concatenate([of_qkv, of_out], axis=1)
        part = mm(grads[r], wq[r], NT)
        part_one = part if part_one is None else part_one + part
        if r:
            last, attn_blocks[r] = hold(last, attn_blocks[r])
            if r == chips - 1:
                last = tie(last, flow_down, flow_up)
    flow_attn = begin(attn_blocks)
    flow_attn[1] = flow_attn[0].send(flow_attn[1])
    part_one = tie(part_one, flow_up, flow_attn)
    back_one, g_gain_one, g_shift_one = norm_back(
        tie(exchange(part_one), flow_down), unit_one, inv_one, gain_one
    )
    input_rows = (d_resid + back_one).astype(BF16)

    def reduce_small():
        shared = jnp.concatenate(
            [
                jnp.sum(da_local, axis=0, dtype=F32),
                g_gain_one,
                g_shift_one,
                g_gain_two,
                g_shift_two,
                jnp.sum(dy_local, axis=0, dtype=F32),
            ]
        )
        if split:
            send = yield shared
            shared = shared + core_swap(send)
        own = []
        for r in range(chips):
            rows_sum = jnp.sum(grads[r], axis=0, dtype=F32)
            hidden_sum = jnp.sum(d_hidden[r], axis=0, dtype=F32)
            own.append(
                jnp.concatenate([shared, hidden_sum, rows_sum[:width], rows_sum[2 * width :]])
            )
        send = yield own[1:]
        vector = own[0]
        for step in steps:
            vector = vector + chip_shift(send[step - 1], chips - step)
        for bit in range(bits):
            send = yield vector
            vector = vector + dp_swap(send, bit)
        return vector

    flow_small = reduce_small()
    flow_small = [flow_small, next(flow_small), None]

    mlp_part = mm(after(acts[0], input_rows), w_down, NN)
    for r in steps:
        mlp_part = mlp_part + mm(acts[r], wd[r], NN)
    keep = own_columns(after(input_rows, mlp_part))
    mlp_part = tie(after(mlp_part, keep), flow_up, flow_attn, flow_small)
    out = (resid + (exchange(mlp_part) + bias_down.astype(F32))).astype(BF16)
    out = tie(out, flow_attn, flow_small)
    keep = [jnp.concatenate(pair, axis=2) for pair in zip(own_columns(out), keep)]
    both = scatter_rows(keep)
    layer_out, input_grad = both[:, :, :width], both[:, :, width:]

    token = tie(after(slot_mask, keep), flow_up, flow_small)
    token = tie(token, flow_attn, flow_small)
    grad_up = finish(flow_up).astype(F32)
    token, grad_up = hold(token, grad_up)
    token = tie(token, flow_attn, flow_small)
    vector = finish(flow_small)
    vecs = [vector[n * full : (n + 1) * full] for n in range(6)]
    mine = vector[6 * full :]

    grad_down = finish(flow_down).astype(F32)
    grad_cat = hold(finish(flow_attn))[0]
    grad_qkv = jnp.stack([grad_cat[:, n * width : (n + 1) * width] for n in range(3)]).astype(F32)
    grad_out = grad_cat[:, 3 * width :].T.astype(F32)
    return (
        layer_out,
        input_grad,
        grad_qkv,
        mine[n_up:].reshape(2, width),
        grad_out,
        vecs[0],
        vecs[1],
        vecs[2],
        vecs[3],
        vecs[4],
        grad_up,
        mine[:n_up],
        grad_down,
        vecs[5],
    )


def solution(mesh):
    return jax.shard_map(
        per_device,
        mesh=mesh,
        in_specs=(
            P("dp", None, "tensor"),
            P("dp", None, "tensor"),
            P("dp"),
            P(None, None, "tensor"),
            P(None, "tensor"),
            P("tensor", None),
            P(),
            P(),
            P(),
            P(),
            P(),
            P(None, "tensor"),
            P("tensor"),
            P("tensor", None),
            P(),
        ),
        out_specs=(
            P("dp", None, "tensor"),
            P("dp", None, "tensor"),
            P(None, None, "tensor"),
            P(None, "tensor"),
            P("tensor", None),
            P(),
            P(),
            P(),
            P(),
            P(),
            P(None, "tensor"),
            P("tensor"),
            P("tensor", None),
            P(),
        ),
        check_vma=False,
    )
```

```python
import functools

import jax
import jax.numpy as jnp
from jax import lax
from jax.experimental import pallas as pl
from jax.experimental.pallas import tpu as pltpu
from jax.sharding import PartitionSpec as P

HEAD = 64
LANES = 128
ROW_TILE = 16
EPS = 1e-05
GELU_K = 1.702
FAR = -1e30

F32 = jnp.float32
BF16 = jnp.bfloat16

NT = (((1,), (1,)), ((), ()))
NN = (((1,), (0,)), ((), ()))
TN = (((0,), (0,)), ((), ()))


def mm(left, right, dims):
    return lax.dot_general(left, right, dims, preferred_element_type=F32)


def head_views(half, seq, q, k):
    lane = lax.broadcasted_iota(jnp.int32, q.shape, 1)
    row = lax.broadcasted_iota(jnp.int32, q.shape, 0)
    mine = (lane >= HEAD) if half else (lane < HEAD)
    spare = lane == (0 if half else HEAD)
    zero = jnp.zeros_like(q)
    q_only = jnp.where(mine, q, zero)
    k_only = jnp.where(mine, k, zero)
    q_mask = jnp.where(spare, jnp.ones_like(q), q_only)
    far = jnp.full_like(k, FAR)
    k_mask = jnp.where(spare & (row >= seq), far, k_only)
    return mine, q_only, k_only, q_mask, k_mask


def attn_fwd_kernel(seq, q_ref, k_ref, v_ref, o_ref, lse_ref):
    q, k, v = q_ref[...], k_ref[...], v_ref[...]
    v_t = v.T
    pieces = []
    for half in range(2):
        _, _, _, q_mask, k_mask = head_views(half, seq, q, k)
        s_t = mm(k_mask, q_mask, NT)
        peak = jnp.max(s_t, axis=0, keepdims=True)
        expo = jnp.exp(s_t - peak)
        total = jnp.sum(expo, axis=0, keepdims=True)
        p_t = (expo * (1.0 / total)).astype(BF16)
        pieces.append(mm(v_t[half * HEAD : (half + 1) * HEAD], p_t, NN))
        lse_ref[0, 0, half : half + 1, :] = peak + jnp.log(total)
    o_ref[...] = jnp.concatenate(pieces, axis=0).T.astype(BF16)


def attn_bwd_kernel(seq, width, q_ref, k_ref, v_ref, do_ref, lse_ref, grads_ref):
    q, k, v, do = q_ref[...], k_ref[...], v_ref[...], do_ref[...]
    k_t = k.T
    dq_t, dk, dv = [], None, None
    for half in range(2):
        mine, q_only, _, q_mask, k_mask = head_views(half, seq, q, k)
        do_only = jnp.where(mine, do, jnp.zeros_like(do))
        s_t = mm(k_mask, q_mask, NT)
        p_t = jnp.exp(s_t - lse_ref[0, 0, half : half + 1, :])
        dp_t = mm(v, do_only, NT)
        inner = jnp.sum(p_t * dp_t, axis=0, keepdims=True)
        ds_t = (p_t * (dp_t - inner)).astype(BF16)
        dv_half = mm(p_t.astype(BF16), do_only, NN)
        dk_half = mm(ds_t, q_only, NN)
        dq_t.append(mm(k_t[half * HEAD : (half + 1) * HEAD], ds_t, NN))
        dv = dv_half if dv is None else dv + dv_half
        dk = dk_half if dk is None else dk + dk_half
    dq = jnp.concatenate(dq_t, axis=0).T.astype(BF16) * 0.125
    for n, grad in enumerate((dq, dk.astype(BF16), dv.astype(BF16))):
        at = pl.multiple_of(n * width + pl.program_id(1) * LANES, LANES)
        grads_ref[:, pl.ds(at, LANES)] = grad


def column_blocks(s, pairs, parts):
    def at(part):
        return pl.BlockSpec((s, LANES), lambda i, j: (i, part * pairs + j))

    return [at(part) for part in range(parts)]


def attention_forward(qkv, images, seq):
    rows, width = qkv.shape[0], qkv.shape[1] // 3
    s = rows // images
    pairs = width // LANES
    block = pl.BlockSpec((s, LANES), lambda i, j: (i, j))
    lse_block = pl.BlockSpec((1, 1, 2, s), lambda i, j: (i, j, 0, 0))
    n = images * pairs * 2
    return pl.pallas_call(
        functools.partial(attn_fwd_kernel, seq),
        grid=(images, pairs),
        in_specs=column_blocks(s, pairs, 3),
        out_specs=[block, lse_block],
        out_shape=[
            jax.ShapeDtypeStruct((rows, width), BF16),
            jax.ShapeDtypeStruct((images, pairs, 2, s), F32),
        ],
        cost_estimate=pl.CostEstimate(
            flops=n * 4 * s * s * 256, bytes_accessed=rows * width * 8, transcendentals=n * s * s
        ),
        name="attn_fwd",
    )(qkv, qkv, qkv)


def attention_backward(qkv, do, lse, images, seq):
    rows, width = do.shape
    s = rows // images
    pairs = width // LANES
    block = pl.BlockSpec((s, LANES), lambda i, j: (i, j))
    lse_block = pl.BlockSpec((1, 1, 2, s), lambda i, j: (i, j, 0, 0))
    n = images * pairs * 2
    return pl.pallas_call(
        functools.partial(attn_bwd_kernel, seq, width),
        grid=(images, pairs),
        in_specs=column_blocks(s, pairs, 3) + [block, lse_block],
        out_specs=pl.BlockSpec((s, 3 * width), lambda i, j: (i, 0)),
        out_shape=jax.ShapeDtypeStruct((rows, 3 * width), BF16),
        cost_estimate=pl.CostEstimate(
            flops=n * 10 * s * s * 256, bytes_accessed=rows * width * 14, transcendentals=n * s * s
        ),
        name="attn_bwd",
    )(qkv, qkv, qkv, do, lse)


def norm_stats(rows):
    mean = jnp.mean(rows, axis=-1, keepdims=True)
    center = rows - mean
    inv = lax.rsqrt(jnp.mean(center * center, axis=-1, keepdims=True) + EPS)
    return mean, inv


def norm_back(grad, unit, inv, gain):
    scaled = grad * gain
    first = jnp.mean(scaled, axis=-1, keepdims=True)
    second = jnp.mean(scaled * unit, axis=-1, keepdims=True)
    return (
        inv * (scaled - first - unit * second),
        jnp.sum(grad * unit, axis=0),
        jnp.sum(grad, axis=0),
    )


def pick(pieces, index):
    out = pieces[0]
    for n in range(1, len(pieces)):
        out = jnp.where(index == n, pieces[n], out)
    return out


def per_device(
    inputs,
    cotangent,
    slot_mask,
    w_qkv,
    bias_qv,
    w_out,
    bias_out,
    ln1_gain,
    ln1_bias,
    ln2_gain,
    ln2_bias,
    w_up,
    bias_up,
    w_down,
    bias_down,
):
    n_img, seq, width = inputs.shape
    n_tensor = lax.axis_size("tensor")
    n_dp = lax.axis_size("dp")
    chips = n_tensor // 2
    images = n_img // chips
    full = width * n_tensor
    padded = -(-seq // ROW_TILE) * ROW_TILE
    split = images % 2 == 0
    near = images // 2 if split else images
    local = near * padded
    t_idx = lax.axis_index("tensor")
    d_idx = lax.axis_index("dp")
    chip, core = t_idx // 2, t_idx % 2
    bits = n_dp.bit_length() - 1
    side = d_idx & 1
    steps = range(1, chips)

    def chip_shift(value, step):
        perm = [
            (2 * a + b, 2 * ((a + step) % chips) + b) for a in range(chips) for b in range(2)
        ]
        return lax.ppermute(value, "tensor", perm)

    def core_swap(value):
        return lax.ppermute(value, "tensor", [(a, a ^ 1) for a in range(n_tensor)])

    def core_trade(value):
        pairs = [[2 * a, 2 * a + 1] for a in range(chips)]
        return lax.all_to_all(value, "tensor", 0, 0, axis_index_groups=pairs)

    def dp_swap(value, bit):
        return lax.ppermute(value, "dp", [(a, a ^ (1 << bit)) for a in range(n_dp)])

    def my_images(value, step):
        return lax.dynamic_slice_in_dim(value, ((chip + step) % chips) * images, images, 0)

    def by_core(first, second):
        return jnp.where(core == 0, first, second)

    def fetch_rows(value):
        return [chip_shift(my_images(value, step), step) for step in steps]

    def core_rows(value, arrived, whole):
        mine = jnp.concatenate([my_images(value, 0)] + arrived, axis=2)
        if split and not whole:
            got = core_swap(by_core(mine[near:], mine[:near]))
            mine = by_core(mine[:near], mine[near:])
        else:
            got = core_swap(mine)
        both = [by_core(mine, got), by_core(got, mine)]
        both = [[b[:, :, a * width : (a + 1) * width] for a in range(chips)] for b in both]
        parts = []
        for a in range(chips):
            parts += [pick(b, (chip - a) % chips) for b in both]
        out = jnp.concatenate(parts, axis=2)
        out = jnp.pad(out, ((0, 0), (0, padded - seq), (0, 0)))
        return out.reshape(-1, full)

    def complete(rows):
        if split:
            rows = core_trade(jnp.broadcast_to(rows, (2,) + rows.shape)).reshape(-1, full)
        return rows

    def exchange(part):
        part = part.astype(BF16)
        if split:
            both = core_trade(part.reshape(2, local, full)).astype(F32)
            return both[0] + both[1]
        return part.astype(F32) + core_swap(part).astype(F32)

    def own_columns(value):
        value = value.reshape(near, padded, full)[:, :seq]
        cols = [value[:, :, n * width : (n + 1) * width] for n in range(n_tensor)]
        cols = [jnp.concatenate(cols[core_of::2], axis=2) for core_of in range(2)]
        if split:
            keep = core_trade(jnp.stack(cols)).reshape(images, seq, chips * width)
        else:
            keep = by_core(*cols)
        return [keep[:, :, a * width : (a + 1) * width] for a in range(chips)]

    def scatter_rows(keep):
        pieces = [pick(keep, chip)]
        for step in steps:
            pieces.append(chip_shift(pick(keep, (chip + step) % chips), step))
        return jnp.concatenate([pick(pieces, (chip - a) % chips) for a in range(chips)], axis=0)

    def my_half(weight):
        half = weight.shape[0] // 2
        return lax.dynamic_slice_in_dim(weight, side * half, half, 0)

    def fetch(send):
        return [chip_shift(send, step) for step in steps]

    def other_halves(arrived):
        return [dp_swap(got, 0) for got in arrived]

    def whole_weight(weight, arrived, others):
        blocks = [weight]
        for got, other in zip(arrived, others):
            block = jnp.where(
                side == 0,
                jnp.concatenate([got, other], 0),
                jnp.concatenate([other, got], 0),
            )
            blocks.append(lax.optimization_barrier(block))
        return blocks

    def halves(value, bit):
        half = value.shape[0] // 2
        at = (d_idx >> bit) & 1
        keep = lax.dynamic_slice_in_dim(value, at * half, half, 0)
        send = lax.dynamic_slice_in_dim(value, (1 - at) * half, half, 0)
        return keep, send

    def add(left, right):
        return (left.astype(F32) + right.astype(F32)).astype(BF16)

    def reduce_blocks(blocks, dp_first):
        first = 0
        if dp_first:
            cut = [halves(block, 0) for block in blocks]
            send = yield [jnp.concatenate([c[1] for c in cut], 0)]
            got = dp_swap(send[0], 0)
            size = cut[0][0].shape[0]
            blocks = [add(c[0], got[n * size : (n + 1) * size]) for n, c in enumerate(cut)]
            first = 1
        send = yield blocks[1:]
        total = blocks[0].astype(F32)
        for step in steps:
            total = total + chip_shift(send[step - 1], chips - step).astype(F32)
        total = total.astype(BF16)
        for bit in range(first, bits - 1):
            keep, send = halves(total, bit)
            send = yield [send]
            total = add(keep, dp_swap(send[0], bit))
        send = yield [total]
        total = add(total, dp_swap(send[0], bits - 1))
        for bit in reversed(range(bits - 1)):
            at = (d_idx >> bit) & 1
            send = yield [total]
            got = dp_swap(send[0], bit)
            if bit == 0:
                total = jnp.concatenate(
                    [jnp.where(at == 0, total, got), jnp.where(at == 0, got, total)], axis=0
                )
                continue
            total = jnp.where(
                at == 0,
                jnp.concatenate([total, got], 0),
                jnp.concatenate([got, total], 0),
            )
        return total

    def begin(blocks, dp_first=False):
        flow = reduce_blocks(blocks, dp_first)
        return [flow, next(flow), None]

    def tie(value, *flows):
        flows = [flow for flow in flows if flow[2] is None]
        value, sends = lax.optimization_barrier((value, [flow[1] for flow in flows]))
        for flow, send in zip(flows, sends):
            advance(flow, send)
        return value

    def advance(flow, send):
        try:
            flow[1] = flow[0].send(send)
        except StopIteration as end:
            flow[1:] = [], end.value

    def finish(flow):
        while flow[2] is None:
            advance(flow, flow[1])
        return flow[2]

    def hold(*values):
        return lax.optimization_barrier(values)

    def after(value, *earlier):
        return lax.optimization_barrier((value, earlier))[0]

    gain_one, shift_one = ln1_gain.astype(F32), ln1_bias.astype(F32)
    gain_two, shift_two = ln2_gain.astype(F32), ln2_bias.astype(F32)

    n_up = bias_up.shape[0]
    small = jnp.concatenate([bias_up, bias_qv.reshape(-1)])
    spare = -small.shape[0] % (ROW_TILE * full)
    small_rows = jnp.pad(small, (0, spare)).reshape(-1, full)
    x_got = fetch_rows(inputs)
    cat_qkv = jnp.concatenate([w_qkv[n] for n in range(3)], axis=1)
    out_rows = jnp.concatenate([my_half(w_out), small_rows], axis=0)
    sends = [my_half(cat_qkv), out_rows, my_half(w_up), my_half(w_down)]
    dy_sends = [my_images(cotangent, step) for step in steps]
    x_got, sends, dy_sends = hold(x_got, sends, dy_sends)
    q_got, o_got, u_got = [fetch(send) for send in sends[:3]]
    scale = jnp.concatenate([jnp.full((width,), 0.125, F32), jnp.ones((2 * width,), F32)])

    def qkv_bias(vector):
        vector = vector[n_up:].astype(F32)
        return jnp.concatenate([vector[:width], jnp.zeros((width,), F32), vector[width:]])

    def project(block, vector):
        return ((mm(normed_one, block, NN) + qkv_bias(vector)) * scale).astype(BF16)

    x32 = core_rows(inputs, x_got, False).astype(F32)
    mean_one, inv_one = norm_stats(x32)
    unit_one = (x32 - mean_one) * inv_one
    normed_one = (unit_one * gain_one + shift_one).astype(BF16)
    normed_one = complete(normed_one)
    qkv = [project(cat_qkv, small)]
    qkv[0], q_got = hold(qkv[0], q_got)
    q_more = other_halves(q_got)
    o, lse = attention_forward(qkv[0], images, seq)
    heads, norms = [o], [lse]
    q_more, o_got = hold(q_more, o_got)
    half_out = w_out.shape[0] // 2
    smalls = [small] + [got[half_out:].reshape(-1)[: small.shape[0]] for got in o_got]
    o_got = [got[:half_out] for got in o_got]
    o_more = other_halves(o_got)
    wq = whole_weight(cat_qkv, q_got, q_more)
    for r in steps:
        qkv.append(project(wq[r], smalls[r]))
    qkv[-1], dy_sends, d_send = hold(qkv[-1], dy_sends, sends[3])
    dy_got = [chip_shift(send, step) for step, send in zip(steps, dy_sends)]
    d_got = fetch(d_send)
    for r in steps:
        o, lse = attention_forward(qkv[r], images, seq)
        heads.append(o)
        norms.append(lse)
    heads[-1], u_got, o_more = hold(heads[-1], u_got, o_more)
    u_more = other_halves(u_got)
    wo = whole_weight(w_out, o_got, o_more)
    attn_part = mm(heads[0], wo[0], NN)
    for r in steps:
        attn_part = attn_part + mm(heads[r], wo[r], NN)
    resid = x32 + (exchange(attn_part) + bias_out.astype(F32))
    mean_two, inv_two = norm_stats(resid)
    unit_two = (resid - mean_two) * inv_two
    normed_two = complete((unit_two * gain_two + shift_two).astype(BF16))
    normed_two, dy_got, u_more = hold(normed_two, dy_got, u_more)

    live = my_images(slot_mask, 0).astype(BF16)
    dy = core_rows(cotangent, dy_got, True).reshape(images, padded, full)
    dy = (dy * live[:, None, None]).reshape(-1, full)
    dy_local = lax.dynamic_slice_in_dim(dy, core * local, local, 0) if split else dy
    acts, slopes = [], []

    def hidden_units(rows, block, vector):
        hidden = mm(rows, block, NN) + vector[:n_up].astype(F32)
        sigma = jax.nn.sigmoid(GELU_K * hidden)
        acts.append((hidden * sigma).astype(BF16))
        slopes.append(sigma + GELU_K * hidden * sigma * (1.0 - sigma))

    hidden_units(normed_two, w_up, small)
    acts[0], dy, d_got = hold(acts[0], dy, d_got)
    d_more = other_halves(d_got)
    wu = whole_weight(w_up, u_got, u_more)
    for r in steps:
        hidden_units(normed_two, wu[r], smalls[r])

    down_sent = [mm(acts[r], dy, TN).astype(BF16) for r in steps]
    first_act, dy, down_sent = lax.optimization_barrier((acts[0], dy, down_sent))
    down_blocks = [mm(first_act, dy, TN).astype(BF16)] + down_sent
    d_hidden = [(mm(dy, w_down, NT) * slopes[0]).astype(BF16)]
    up_blocks = [mm(normed_two, d_hidden[0], TN).astype(BF16)]
    part_two = mm(d_hidden[0], w_up, NT)
    up_blocks[0], down_blocks[0], part_two, d_more = hold(
        up_blocks[0], down_blocks[0], part_two, d_more
    )
    wd = whole_weight(w_down, d_got, d_more)
    for r in steps:
        d_hidden.append((mm(dy, wd[r], NT) * slopes[r]).astype(BF16))
        up_blocks.append(mm(normed_two, d_hidden[r], TN).astype(BF16))
    d_hidden, up_blocks = lax.optimization_barrier((d_hidden, up_blocks))
    flow_down = begin(down_blocks)
    flow_up = begin(up_blocks)
    flow_down[1] = flow_down[0].send(flow_down[1])
    flow_up[1] = flow_up[0].send(flow_up[1])
    for r in steps:
        part_two = part_two + mm(d_hidden[r], wu[r], NT)
    back_two, g_gain_two, g_shift_two = norm_back(exchange(part_two), unit_two, inv_two, gain_two)
    d_resid = dy_local.astype(F32) + back_two
    da_local = d_resid.astype(BF16)
    da = tie(complete(da_local), flow_down)

    grads, attn_blocks = [None] * chips, [None] * chips
    part_one = None
    last = da
    for r in list(steps) + [0]:
        do = mm(last, wo[r], NT).astype(BF16)
        grads[r] = attention_backward(qkv[r], do, norms[r], images, seq)
        if r == chips - 1:
            grads[r] = tie(grads[r], flow_down)
        if r == 0:
            grads[r] = tie(grads[r], flow_up, flow_down)
        of_qkv = mm(normed_one, grads[r], TN).astype(BF16)
        of_out = mm(da, after(heads[r], grads[r]), TN).astype(BF16)
        attn_blocks[r] = jnp.concatenate([of_qkv, of_out], axis=1)
        part = mm(grads[r], wq[r], NT)
        part_one = part if part_one is None else part_one + part
        if r:
            last, attn_blocks[r] = hold(last, attn_blocks[r])
            if r == chips - 1:
                last = tie(last, flow_down, flow_up)
    flow_attn = begin(attn_blocks)
    flow_attn[1] = flow_attn[0].send(flow_attn[1])
    part_one = tie(part_one, flow_up, flow_attn)
    back_one, g_gain_one, g_shift_one = norm_back(
        tie(exchange(part_one), flow_down), unit_one, inv_one, gain_one
    )
    input_rows = (d_resid + back_one).astype(BF16)

    def reduce_small():
        shared = jnp.concatenate(
            [
                jnp.sum(da_local, axis=0, dtype=F32),
                g_gain_one,
                g_shift_one,
                g_gain_two,
                g_shift_two,
                jnp.sum(dy_local, axis=0, dtype=F32),
            ]
        )
        if split:
            send = yield shared
            shared = shared + core_swap(send)
        own = []
        for r in range(chips):
            rows_sum = jnp.sum(grads[r], axis=0, dtype=F32)
            hidden_sum = jnp.sum(d_hidden[r], axis=0, dtype=F32)
            own.append(
                jnp.concatenate([shared, hidden_sum, rows_sum[:width], rows_sum[2 * width :]])
            )
        send = yield own[1:]
        vector = own[0]
        for step in steps:
            vector = vector + chip_shift(send[step - 1], chips - step)
        for bit in range(bits):
            send = yield vector
            vector = vector + dp_swap(send, bit)
        return vector

    flow_small = reduce_small()
    flow_small = [flow_small, next(flow_small), None]

    mlp_part = mm(after(acts[0], input_rows), w_down, NN)
    for r in steps:
        mlp_part = mlp_part + mm(acts[r], wd[r], NN)
    keep = own_columns(after(input_rows, mlp_part))
    mlp_part = tie(after(mlp_part, keep), flow_up, flow_attn, flow_small)
    out = (resid + (exchange(mlp_part) + bias_down.astype(F32))).astype(BF16)
    out = tie(out, flow_attn, flow_small)
    keep = [jnp.concatenate(pair, axis=2) for pair in zip(own_columns(out), keep)]
    both = scatter_rows(keep)
    layer_out, input_grad = both[:, :, :width], both[:, :, width:]

    token = tie(after(slot_mask, keep), flow_up, flow_small)
    token = tie(token, flow_attn, flow_small)
    grad_up = finish(flow_up).astype(F32)
    token, grad_up = hold(token, grad_up)
    token = tie(token, flow_attn, flow_small)
    vector = finish(flow_small)
    vecs = [vector[n * full : (n + 1) * full] for n in range(6)]
    mine = vector[6 * full :]

    grad_down = finish(flow_down).astype(F32)
    grad_cat = hold(finish(flow_attn))[0]
    grad_qkv = jnp.stack([grad_cat[:, n * width : (n + 1) * width] for n in range(3)]).astype(F32)
    grad_out = grad_cat[:, 3 * width :].T.astype(F32)
    return (
        layer_out,
        input_grad,
        grad_qkv,
        mine[n_up:].reshape(2, width),
        grad_out,
        vecs[0],
        vecs[1],
        vecs[2],
        vecs[3],
        vecs[4],
        grad_up,
        mine[:n_up],
        grad_down,
        vecs[5],
    )


def solution(mesh):
    return jax.shard_map(
        per_device,
        mesh=mesh,
        in_specs=(
            P("dp", None, "tensor"),
            P("dp", None, "tensor"),
            P("dp"),
            P(None, None, "tensor"),
            P(None, "tensor"),
            P("tensor", None),
            P(),
            P(),
            P(),
            P(),
            P(),
            P(None, "tensor"),
            P("tensor"),
            P("tensor", None),
            P(),
        ),
        out_specs=(
            P("dp", None, "tensor"),
            P("dp", None, "tensor"),
            P(None, None, "tensor"),
            P(None, "tensor"),
            P("tensor", None),
            P(),
            P(),
            P(),
            P(),
            P(),
            P(None, "tensor"),
            P("tensor"),
            P("tensor", None),
            P(),
        ),
        check_vma=False,
    )
```

```python
import functools

import jax
import jax.numpy as jnp
from jax import lax
from jax.experimental import pallas as pl
from jax.experimental.pallas import tpu as pltpu
from jax.sharding import PartitionSpec as P

HEAD = 64
LANES = 128
ROW_TILE = 16
EPS = 1e-05
GELU_K = 1.702
FAR = -1e30

F32 = jnp.float32
BF16 = jnp.bfloat16

NT = (((1,), (1,)), ((), ()))
NN = (((1,), (0,)), ((), ()))
TN = (((0,), (0,)), ((), ()))


def mm(left, right, dims):
    return lax.dot_general(left, right, dims, preferred_element_type=F32)


def head_views(half, seq, q, k):
    lane = lax.broadcasted_iota(jnp.int32, q.shape, 1)
    row = lax.broadcasted_iota(jnp.int32, q.shape, 0)
    mine = (lane >= HEAD) if half else (lane < HEAD)
    spare = lane == (0 if half else HEAD)
    zero = jnp.zeros_like(q)
    q_only = jnp.where(mine, q, zero)
    k_only = jnp.where(mine, k, zero)
    q_mask = jnp.where(spare, jnp.ones_like(q), q_only)
    far = jnp.full_like(k, FAR)
    k_mask = jnp.where(spare & (row >= seq), far, k_only)
    return mine, q_only, k_only, q_mask, k_mask


def attn_fwd_kernel(seq, q_ref, k_ref, v_ref, o_ref, lse_ref):
    q, k, v = q_ref[...], k_ref[...], v_ref[...]
    v_t = v.T
    pieces = []
    for half in range(2):
        _, _, _, q_mask, k_mask = head_views(half, seq, q, k)
        s_t = mm(k_mask, q_mask, NT)
        peak = jnp.max(s_t, axis=0, keepdims=True)
        expo = jnp.exp(s_t - peak)
        total = jnp.sum(expo, axis=0, keepdims=True)
        p_t = (expo * (1.0 / total)).astype(BF16)
        pieces.append(mm(v_t[half * HEAD : (half + 1) * HEAD], p_t, NN))
        lse_ref[0, 0, half : half + 1, :] = peak + jnp.log(total)
    o_ref[...] = jnp.concatenate(pieces, axis=0).T.astype(BF16)


def attn_bwd_kernel(seq, width, q_ref, k_ref, v_ref, do_ref, lse_ref, grads_ref):
    q, k, v, do = q_ref[...], k_ref[...], v_ref[...], do_ref[...]
    k_t = k.T
    dq_t, dk, dv = [], None, None
    for half in range(2):
        mine, q_only, _, q_mask, k_mask = head_views(half, seq, q, k)
        do_only = jnp.where(mine, do, jnp.zeros_like(do))
        s_t = mm(k_mask, q_mask, NT)
        p_t = jnp.exp(s_t - lse_ref[0, 0, half : half + 1, :])
        dp_t = mm(v, do_only, NT)
        inner = jnp.sum(p_t * dp_t, axis=0, keepdims=True)
        ds_t = (p_t * (dp_t - inner)).astype(BF16)
        dv_half = mm(p_t.astype(BF16), do_only, NN)
        dk_half = mm(ds_t, q_only, NN)
        dq_t.append(mm(k_t[half * HEAD : (half + 1) * HEAD], ds_t, NN))
        dv = dv_half if dv is None else dv + dv_half
        dk = dk_half if dk is None else dk + dk_half
    dq = jnp.concatenate(dq_t, axis=0).T.astype(BF16) * 0.125
    for n, grad in enumerate((dq, dk.astype(BF16), dv.astype(BF16))):
        at = pl.multiple_of(n * width + pl.program_id(1) * LANES, LANES)
        grads_ref[:, pl.ds(at, LANES)] = grad


def column_blocks(s, pairs, parts):
    def at(part):
        return pl.BlockSpec((s, LANES), lambda i, j: (i, part * pairs + j))

    return [at(part) for part in range(parts)]


def attention_forward(qkv, images, seq):
    rows, width = qkv.shape[0], qkv.shape[1] // 3
    s = rows // images
    pairs = width // LANES
    block = pl.BlockSpec((s, LANES), lambda i, j: (i, j))
    lse_block = pl.BlockSpec((1, 1, 2, s), lambda i, j: (i, j, 0, 0))
    n = images * pairs * 2
    return pl.pallas_call(
        functools.partial(attn_fwd_kernel, seq),
        grid=(images, pairs),
        in_specs=column_blocks(s, pairs, 3),
        out_specs=[block, lse_block],
        out_shape=[
            jax.ShapeDtypeStruct((rows, width), BF16),
            jax.ShapeDtypeStruct((images, pairs, 2, s), F32),
        ],
        cost_estimate=pl.CostEstimate(
            flops=n * 4 * s * s * 256, bytes_accessed=rows * width * 8, transcendentals=n * s * s
        ),
        name="attn_fwd",
    )(qkv, qkv, qkv)


def attention_backward(qkv, do, lse, images, seq):
    rows, width = do.shape
    s = rows // images
    pairs = width // LANES
    block = pl.BlockSpec((s, LANES), lambda i, j: (i, j))
    lse_block = pl.BlockSpec((1, 1, 2, s), lambda i, j: (i, j, 0, 0))
    n = images * pairs * 2
    return pl.pallas_call(
        functools.partial(attn_bwd_kernel, seq, width),
        grid=(images, pairs),
        in_specs=column_blocks(s, pairs, 3) + [block, lse_block],
        out_specs=pl.BlockSpec((s, 3 * width), lambda i, j: (i, 0)),
        out_shape=jax.ShapeDtypeStruct((rows, 3 * width), BF16),
        cost_estimate=pl.CostEstimate(
            flops=n * 10 * s * s * 256, bytes_accessed=rows * width * 14, transcendentals=n * s * s
        ),
        name="attn_bwd",
    )(qkv, qkv, qkv, do, lse)


def norm_stats(rows):
    mean = jnp.mean(rows, axis=-1, keepdims=True)
    center = rows - mean
    inv = lax.rsqrt(jnp.mean(center * center, axis=-1, keepdims=True) + EPS)
    return mean, inv


def norm_back(grad, unit, inv, gain):
    scaled = grad * gain
    first = jnp.mean(scaled, axis=-1, keepdims=True)
    second = jnp.mean(scaled * unit, axis=-1, keepdims=True)
    return (
        inv * (scaled - first - unit * second),
        jnp.sum(grad * unit, axis=0),
        jnp.sum(grad, axis=0),
    )


def pick(pieces, index):
    out = pieces[0]
    for n in range(1, len(pieces)):
        out = jnp.where(index == n, pieces[n], out)
    return out


def per_device(
    inputs,
    cotangent,
    slot_mask,
    w_qkv,
    bias_qv,
    w_out,
    bias_out,
    ln1_gain,
    ln1_bias,
    ln2_gain,
    ln2_bias,
    w_up,
    bias_up,
    w_down,
    bias_down,
):
    n_img, seq, width = inputs.shape
    n_tensor = lax.axis_size("tensor")
    n_dp = lax.axis_size("dp")
    chips = n_tensor // 2
    images = n_img // chips
    full = width * n_tensor
    padded = -(-seq // ROW_TILE) * ROW_TILE
    split = images % 2 == 0
    near = images // 2 if split else images
    local = near * padded
    t_idx = lax.axis_index("tensor")
    d_idx = lax.axis_index("dp")
    chip, core = t_idx // 2, t_idx % 2
    bits = n_dp.bit_length() - 1
    side = d_idx & 1
    steps = range(1, chips)

    def chip_shift(value, step):
        perm = [
            (2 * a + b, 2 * ((a + step) % chips) + b) for a in range(chips) for b in range(2)
        ]
        return lax.ppermute(value, "tensor", perm)

    def core_swap(value):
        return lax.ppermute(value, "tensor", [(a, a ^ 1) for a in range(n_tensor)])

    def core_trade(value):
        pairs = [[2 * a, 2 * a + 1] for a in range(chips)]
        return lax.all_to_all(value, "tensor", 0, 0, axis_index_groups=pairs)

    def dp_swap(value, bit):
        return lax.ppermute(value, "dp", [(a, a ^ (1 << bit)) for a in range(n_dp)])

    def my_images(value, step):
        return lax.dynamic_slice_in_dim(value, ((chip + step) % chips) * images, images, 0)

    def by_core(first, second):
        return jnp.where(core == 0, first, second)

    def fetch_rows(value):
        return [chip_shift(my_images(value, step), step) for step in steps]

    def core_rows(value, arrived, whole):
        mine = jnp.concatenate([my_images(value, 0)] + arrived, axis=2)
        if split and not whole:
            got = core_swap(by_core(mine[near:], mine[:near]))
            mine = by_core(mine[:near], mine[near:])
        else:
            got = core_swap(mine)
        both = [by_core(mine, got), by_core(got, mine)]
        both = [[b[:, :, a * width : (a + 1) * width] for a in range(chips)] for b in both]
        parts = []
        for a in range(chips):
            parts += [pick(b, (chip - a) % chips) for b in both]
        out = jnp.concatenate(parts, axis=2)
        out = jnp.pad(out, ((0, 0), (0, padded - seq), (0, 0)))
        return out.reshape(-1, full)

    def complete(rows):
        if split:
            rows = core_trade(jnp.broadcast_to(rows, (2,) + rows.shape)).reshape(-1, full)
        return rows

    def exchange(part):
        part = part.astype(BF16)
        if split:
            both = core_trade(part.reshape(2, local, full)).astype(F32)
            return both[0] + both[1]
        return part.astype(F32) + core_swap(part).astype(F32)

    def own_columns(value):
        value = value.reshape(near, padded, full)[:, :seq]
        cols = [value[:, :, n * width : (n + 1) * width] for n in range(n_tensor)]
        cols = [jnp.concatenate(cols[core_of::2], axis=2) for core_of in range(2)]
        if split:
            keep = core_trade(jnp.stack(cols)).reshape(images, seq, chips * width)
        else:
            keep = by_core(*cols)
        return [keep[:, :, a * width : (a + 1) * width] for a in range(chips)]

    def scatter_rows(keep):
        pieces = [pick(keep, chip)]
        for step in steps:
            pieces.append(chip_shift(pick(keep, (chip + step) % chips), step))
        return jnp.concatenate([pick(pieces, (chip - a) % chips) for a in range(chips)], axis=0)

    def my_half(weight):
        half = weight.shape[0] // 2
        return lax.dynamic_slice_in_dim(weight, side * half, half, 0)

    def fetch(send):
        return [chip_shift(send, step) for step in steps]

    def other_halves(arrived):
        return [dp_swap(got, 0) for got in arrived]

    def whole_weight(weight, arrived, others):
        blocks = [weight]
        for got, other in zip(arrived, others):
            block = jnp.where(
                side == 0,
                jnp.concatenate([got, other], 0),
                jnp.concatenate([other, got], 0),
            )
            blocks.append(lax.optimization_barrier(block))
        return blocks

    def halves(value, bit):
        half = value.shape[0] // 2
        at = (d_idx >> bit) & 1
        keep = lax.dynamic_slice_in_dim(value, at * half, half, 0)
        send = lax.dynamic_slice_in_dim(value, (1 - at) * half, half, 0)
        return keep, send

    def add(left, right):
        return (left.astype(F32) + right.astype(F32)).astype(BF16)

    def reduce_blocks(blocks):
        send = yield blocks[1:]
        got = [chip_shift(send[step - 1], chips - step) for step in steps]
        total = (yield blocks[0]).astype(F32)
        for piece in got:
            total = total + piece.astype(F32)
        total = total.astype(BF16)
        for bit in range(bits - 1):
            keep, send = halves(total, bit)
            send = yield send
            got = dp_swap(send, bit)
            keep = yield keep
            total = add(keep, got)
        send = yield total
        got = dp_swap(send, bits - 1)
        keep = yield total
        total = add(keep, got)
        for bit in reversed(range(bits - 1)):
            at = (d_idx >> bit) & 1
            send = yield total
            got = dp_swap(send, bit)
            total = yield total
            if bit == 0:
                total = jnp.concatenate(
                    [jnp.where(at == 0, total, got), jnp.where(at == 0, got, total)], axis=0
                )
                continue
            total = jnp.where(
                at == 0,
                jnp.concatenate([total, got], 0),
                jnp.concatenate([got, total], 0),
            )
        return total

    def begin(flow):
        return [flow, flow.send(next(flow)), None]

    def advance(flow):
        try:
            flow[1] = flow[0].send(flow[1])
        except StopIteration as end:
            flow[1:] = [], end.value

    def tie(value, *flows):
        for phase in range(2):
            going = [flow for flow in flows if flow[2] is None]
            value, held = lax.optimization_barrier((value, [flow[1] for flow in going]))
            for flow, item in zip(going, held):
                flow[1] = item
                advance(flow)
        return value

    def finish(flow):
        while flow[2] is None:
            advance(flow)
        return flow[2]

    def hold(*values):
        return lax.optimization_barrier(values)

    def after(value, *earlier):
        return lax.optimization_barrier((value, earlier))[0]

    gain_one, shift_one = ln1_gain.astype(F32), ln1_bias.astype(F32)
    gain_two, shift_two = ln2_gain.astype(F32), ln2_bias.astype(F32)

    n_up = bias_up.shape[0]
    small = jnp.concatenate([bias_up, bias_qv.reshape(-1)])
    spare = -small.shape[0] % (ROW_TILE * full)
    small_rows = jnp.pad(small, (0, spare)).reshape(-1, full)
    x_got = fetch_rows(inputs)
    cat_qkv = jnp.concatenate([w_qkv[n] for n in range(3)], axis=1)
    out_rows = jnp.concatenate([my_half(w_out), small_rows], axis=0)
    sends = [my_half(cat_qkv), out_rows, my_half(w_up), my_half(w_down)]
    dy_sends = [my_images(cotangent, step) for step in steps]
    x_got, sends, dy_sends = hold(x_got, sends, dy_sends)
    q_got, o_got, u_got = [fetch(send) for send in sends[:3]]
    scale = jnp.concatenate([jnp.full((width,), 0.125, F32), jnp.ones((2 * width,), F32)])

    def qkv_bias(vector):
        vector = vector[n_up:].astype(F32)
        return jnp.concatenate([vector[:width], jnp.zeros((width,), F32), vector[width:]])

    def project(block, vector):
        return ((mm(normed_one, block, NN) + qkv_bias(vector)) * scale).astype(BF16)

    x32 = core_rows(inputs, x_got, False).astype(F32)
    mean_one, inv_one = norm_stats(x32)
    unit_one = (x32 - mean_one) * inv_one
    normed_one = (unit_one * gain_one + shift_one).astype(BF16)
    normed_one = complete(normed_one)
    qkv = [project(cat_qkv, small)]
    qkv[0], q_got = hold(qkv[0], q_got)
    q_more = other_halves(q_got)
    o, lse = attention_forward(qkv[0], images, seq)
    heads, norms = [o], [lse]
    q_more, o_got = hold(q_more, o_got)
    half_out = w_out.shape[0] // 2
    smalls = [small] + [got[half_out:].reshape(-1)[: small.shape[0]] for got in o_got]
    o_got = [got[:half_out] for got in o_got]
    o_more = other_halves(o_got)
    wq = whole_weight(cat_qkv, q_got, q_more)
    for r in steps:
        qkv.append(project(wq[r], smalls[r]))
    qkv[-1], dy_sends, d_send = hold(qkv[-1], dy_sends, sends[3])
    dy_got = [chip_shift(send, step) for step, send in zip(steps, dy_sends)]
    d_got = fetch(d_send)
    for r in steps:
        o, lse = attention_forward(qkv[r], images, seq)
        heads.append(o)
        norms.append(lse)
    heads[-1], u_got, o_more = hold(heads[-1], u_got, o_more)
    u_more = other_halves(u_got)
    wo = whole_weight(w_out, o_got, o_more)
    attn_part = mm(heads[0], wo[0], NN)
    for r in steps:
        attn_part = attn_part + mm(heads[r], wo[r], NN)
    resid = x32 + (exchange(attn_part) + bias_out.astype(F32))
    mean_two, inv_two = norm_stats(resid)
    unit_two = (resid - mean_two) * inv_two
    normed_two = complete((unit_two * gain_two + shift_two).astype(BF16))
    normed_two, dy_got, u_more = hold(normed_two, dy_got, u_more)

    live = my_images(slot_mask, 0).astype(BF16)
    dy = core_rows(cotangent, dy_got, True).reshape(images, padded, full)
    dy = (dy * live[:, None, None]).reshape(-1, full)
    dy_local = lax.dynamic_slice_in_dim(dy, core * local, local, 0) if split else dy
    acts, slopes = [], []

    def hidden_units(rows, block, vector):
        hidden = mm(rows, block, NN) + vector[:n_up].astype(F32)
        sigma = jax.nn.sigmoid(GELU_K * hidden)
        acts.append((hidden * sigma).astype(BF16))
        slopes.append(sigma + GELU_K * hidden * sigma * (1.0 - sigma))

    hidden_units(normed_two, w_up, small)
    acts[0], dy, d_got = hold(acts[0], dy, d_got)
    d_more = other_halves(d_got)
    wu = whole_weight(w_up, u_got, u_more)
    for r in steps:
        hidden_units(normed_two, wu[r], smalls[r])

    down_sent = [mm(acts[r], dy, TN).astype(BF16) for r in steps]
    first_act, dy, down_sent = lax.optimization_barrier((acts[0], dy, down_sent))
    down_blocks = [mm(first_act, dy, TN).astype(BF16)] + down_sent
    d_hidden = [(mm(dy, w_down, NT) * slopes[0]).astype(BF16)]
    up_blocks = [mm(normed_two, d_hidden[0], TN).astype(BF16)]
    part_two = mm(d_hidden[0], w_up, NT)
    up_blocks[0], down_blocks[0], part_two, d_more = hold(
        up_blocks[0], down_blocks[0], part_two, d_more
    )
    wd = whole_weight(w_down, d_got, d_more)
    for r in steps:
        d_hidden.append((mm(dy, wd[r], NT) * slopes[r]).astype(BF16))
        up_blocks.append(mm(normed_two, d_hidden[r], TN).astype(BF16))
    d_hidden, up_blocks = lax.optimization_barrier((d_hidden, up_blocks))
    flow_down = begin(reduce_blocks(down_blocks))
    flow_up = begin(reduce_blocks(up_blocks))
    for r in steps:
        part_two = part_two + mm(d_hidden[r], wu[r], NT)
    back_two, g_gain_two, g_shift_two = norm_back(exchange(part_two), unit_two, inv_two, gain_two)
    d_resid = dy_local.astype(F32) + back_two
    da_local = d_resid.astype(BF16)
    da = tie(complete(da_local), flow_down)

    grads, attn_blocks = [None] * chips, [None] * chips
    part_one = None
    last = da
    for r in list(steps) + [0]:
        do = mm(last, wo[r], NT).astype(BF16)
        grads[r] = attention_backward(qkv[r], do, norms[r], images, seq)
        if r == chips - 1:
            grads[r] = tie(grads[r], flow_down)
        if r == 0:
            grads[r] = tie(grads[r], flow_up, flow_down)
        of_qkv = mm(normed_one, grads[r], TN).astype(BF16)
        of_out = mm(da, after(heads[r], grads[r]), TN).astype(BF16)
        attn_blocks[r] = jnp.concatenate([of_qkv, of_out], axis=1)
        part = mm(grads[r], wq[r], NT)
        part_one = part if part_one is None else part_one + part
        if r:
            last, attn_blocks[r] = hold(last, attn_blocks[r])
            if r == chips - 1:
                last = tie(last, flow_down, flow_up)
    flow_attn = begin(reduce_blocks(attn_blocks))
    part_one = tie(part_one, flow_up, flow_attn)
    back_one, g_gain_one, g_shift_one = norm_back(
        tie(exchange(part_one), flow_down), unit_one, inv_one, gain_one
    )
    input_rows = (d_resid + back_one).astype(BF16)

    def reduce_small():
        shared = jnp.concatenate(
            [
                jnp.sum(da_local, axis=0, dtype=F32),
                g_gain_one,
                g_shift_one,
                g_gain_two,
                g_shift_two,
                jnp.sum(dy_local, axis=0, dtype=F32),
            ]
        )
        if split:
            send = yield shared
            got = core_swap(send)
            shared = (yield shared) + got
        own = []
        for r in range(chips):
            rows_sum = jnp.sum(grads[r], axis=0, dtype=F32)
            hidden_sum = jnp.sum(d_hidden[r], axis=0, dtype=F32)
            own.append(
                jnp.concatenate([shared, hidden_sum, rows_sum[:width], rows_sum[2 * width :]])
            )
        send = yield own[1:]
        got = [chip_shift(send[step - 1], chips - step) for step in steps]
        vector = yield own[0]
        for piece in got:
            vector = vector + piece
        for bit in list(range(1, bits)) + [0]:
            send = yield vector
            got = dp_swap(send, bit)
            vector = (yield vector) + got
        return vector

    flow_small = begin(reduce_small())

    mlp_part = mm(after(acts[0], input_rows), w_down, NN)
    for r in steps:
        mlp_part = mlp_part + mm(acts[r], wd[r], NN)
    keep = own_columns(after(input_rows, mlp_part))
    mlp_part = tie(after(mlp_part, keep), flow_up, flow_attn, flow_small)
    out = (resid + (exchange(mlp_part) + bias_down.astype(F32))).astype(BF16)
    out = tie(out, flow_attn, flow_small)
    token = tie(after(slot_mask, out), flow_up)
    token, out = hold(token, out)
    keep = [jnp.concatenate(pair, axis=2) for pair in zip(own_columns(out), keep)]
    both = scatter_rows(keep)
    layer_out, input_grad = both[:, :, :width], both[:, :, width:]

    token = tie(after(token, keep), flow_small)
    token = tie(token, flow_attn, flow_small)
    grad_up = finish(flow_up).astype(F32)
    token, grad_up = hold(token, grad_up)
    token = tie(token, flow_small)
    token = tie(token, flow_attn)
    vector = finish(flow_small)
    vecs = [vector[n * full : (n + 1) * full] for n in range(6)]
    mine = vector[6 * full :]

    grad_down = finish(flow_down).astype(F32)
    grad_cat = hold(finish(flow_attn))[0]
    grad_qkv = jnp.stack([grad_cat[:, n * width : (n + 1) * width] for n in range(3)]).astype(F32)
    grad_out = grad_cat[:, 3 * width :].T.astype(F32)
    return (
        layer_out,
        input_grad,
        grad_qkv,
        mine[n_up:].reshape(2, width),
        grad_out,
        vecs[0],
        vecs[1],
        vecs[2],
        vecs[3],
        vecs[4],
        grad_up,
        mine[:n_up],
        grad_down,
        vecs[5],
    )


def solution(mesh):
    return jax.shard_map(
        per_device,
        mesh=mesh,
        in_specs=(
            P("dp", None, "tensor"),
            P("dp", None, "tensor"),
            P("dp"),
            P(None, None, "tensor"),
            P(None, "tensor"),
            P("tensor", None),
            P(),
            P(),
            P(),
            P(),
            P(),
            P(None, "tensor"),
            P("tensor"),
            P("tensor", None),
            P(),
        ),
        out_specs=(
            P("dp", None, "tensor"),
            P("dp", None, "tensor"),
            P(None, None, "tensor"),
            P(None, "tensor"),
            P("tensor", None),
            P(),
            P(),
            P(),
            P(),
            P(),
            P(None, "tensor"),
            P("tensor"),
            P("tensor", None),
            P(),
        ),
        check_vma=False,
    )
```
